512 devices in a mesh: row: 16 (over y, z_hi), col: 32 (over z_lo, x, core).
Axes of the slice: x: 4, y: 4, z: 16 (z_hi: 4, z_lo: 4; z = z_hi * 4 + z_lo), core: 2. Of those that a mesh axis runs over, the one named last changes fastest.
Arguments:
- queries: bfloat16 [16384, 768], P(('row', 'col')), may hold values from -8 to 8
- tools: bfloat16 [24576, 768], P(('col', 'row')), may hold values from -8 to 8
- query_mass: float32 [16384], P('row'), may hold values from 0.5 to 5
- tool_mass: float32 [24576], P('col'), may hold values from 0.5 to 5
Outputs:
- mapped_queries: bfloat16 [16384, 768], P(('row', 'col'))
- query_potential: float32 [16384], P('row')
- tool_potential: float32 [24576], P('col')
The draws below stay inside these ranges and needn't reach their ends.
All inputs are finite; a program needn't handle non-finite values.
Results may differ from the reference program's by a relative error of at most 0.0025.
Values may be sent and summed in bfloat16 or wider, within the bound.
A program may use at most 64 MiB of HBM per device.

```python
import math
import jax
import jax.numpy as jnp
from jax import lax

D = 768
QR_DEV = 1024
ITERS = 3
NQ = 16384
NT = 24576


def embed_draw(key):
    query_key = jax.random.fold_in(key, 101)
    tool_key = jax.random.fold_in(key, 202)
    sign_key = jax.random.fold_in(key, 606)
    half_width = D // 2
    sign_pattern = (jax.random.randint(sign_key, (D,), 0, 2) * 2 - 1).astype(jnp.float32)
    first_half = jnp.arange(D) < half_width
    query_common = jnp.where(first_half, sign_pattern, 0.0)
    tool_common = jnp.where(first_half, 0.0, sign_pattern)
    queries = jax.random.truncated_normal(query_key, -6.0, 6.0, (NQ, D), jnp.float32)
    tools = jax.random.truncated_normal(tool_key, -6.0, 6.0, (NT, D), jnp.float32)
    queries = queries + query_common[None, :]
    tools = tools + tool_common[None, :]
    for block_index in (1, 3, 5):
        far_query = block_index * (NQ // 6) + NQ // 12
        far_tool = block_index * (NT // 6) + NT // 12
        queries = queries.at[far_query].set(jnp.where(first_half, queries[far_query], -8.0 * tool_common))
        tools = tools.at[far_tool].set(jnp.where(first_half, -8.0 * query_common, tools[far_tool]))
    return (queries, tools)


def draw_queries(key, part):
    return embed_draw(key)[0].astype(jnp.bfloat16)


def draw_tools(key, part):
    return embed_draw(key)[1].astype(jnp.bfloat16)


def draw_query_mass(key, part):
    position = jnp.arange(NQ, dtype=jnp.float32) / NQ
    noise = jax.random.uniform(jax.random.fold_in(key, 404), (NQ,), jnp.float32, -0.5, 0.5)
    return jnp.exp(noise) * jnp.exp(position * 1.0986123)


def draw_tool_mass(key, part):
    position = jnp.arange(NT, dtype=jnp.float32) / NT
    noise = jax.random.uniform(jax.random.fold_in(key, 505), (NT,), jnp.float32, -0.5, 0.5)
    return jnp.exp(noise) * jnp.exp(position * 1.0986123)


def setup_inputs(seed: int = 0) -> dict:
    seeds = jax.random.split(jax.random.key(seed), 5)
    queries = draw_queries(jax.random.fold_in(seeds[4], 71), 0)
    tools = draw_tools(jax.random.fold_in(seeds[4], 71), 0)
    query_mass = draw_query_mass(jax.random.fold_in(seeds[4], 71), 0)
    tool_mass = draw_tool_mass(jax.random.fold_in(seeds[4], 71), 0)
    return {"queries": queries, "tools": tools, "query_mass": query_mass, "tool_mass": tool_mass}


EPSILON = 0.5

def cost_block(query_block, tools):
    products = jnp.dot(query_block, tools.T, preferred_element_type=jnp.float32)
    return products * (-1.0 / math.sqrt(D))

def reference(queries, tools, query_mass, tool_mass):
    query_blocks = queries.reshape(NQ // QR_DEV, QR_DEV, D)
    log_query = jnp.log(query_mass)
    log_tool = jnp.log(tool_mass)

    def row_pass(tool_potential):

        def one_block(query_block):
            scores = (tool_potential[None, :] - cost_block(query_block, tools)) / EPSILON
            maxima = lax.optimization_barrier(jnp.max(scores, axis=1))
            return maxima + jnp.log(lax.optimization_barrier(jnp.sum(jnp.exp(scores - maxima[:, None]), axis=1)))
        return lax.map(one_block, query_blocks).reshape(NQ)

    def column_pass(query_potential):
        potential_blocks = query_potential.reshape(NQ // QR_DEV, QR_DEV)

        def advance(running, element):
            query_block, potential_block = element
            scores = (potential_block[:, None] - cost_block(query_block, tools)) / EPSILON
            highest = jnp.maximum(running[0], lax.optimization_barrier(jnp.max(scores, axis=0)))
            summed = running[1] * jnp.exp(running[0] - highest) + lax.optimization_barrier(jnp.sum(jnp.exp(scores - highest[None, :]), axis=0))
            return ((highest, summed), None)
        start_state = (jnp.full((NT,), -jnp.inf, jnp.float32), jnp.zeros((NT,), jnp.float32))
        final_state, unused = lax.scan(advance, start_state, (query_blocks, potential_blocks))
        return final_state[0] + jnp.log(final_state[1])
    tool_potential = jnp.zeros((NT,), jnp.float32)
    query_potential = jnp.zeros((NQ,), jnp.float32)
    for sweep in range(ITERS):
        query_potential = EPSILON * log_query - EPSILON * row_pass(tool_potential)
        tool_potential = EPSILON * log_tool - EPSILON * column_pass(query_potential)

    def map_block(query_block):
        scores = (tool_potential[None, :] - cost_block(query_block, tools)) / EPSILON
        peaks = lax.optimization_barrier(jnp.max(scores, axis=1))
        exps = jnp.exp(scores - peaks[:, None])
        totals = lax.optimization_barrier(jnp.sum(exps, axis=1))
        weights = exps.astype(jnp.bfloat16)
        summed = jnp.dot(weights, tools, preferred_element_type=jnp.float32)
        return (summed / totals[:, None]).astype(jnp.bfloat16)
    mapped_queries = lax.map(map_block, query_blocks).reshape(NQ, D)
    return (mapped_queries, query_potential, tool_potential)
```

```python
import math

import jax
import jax.numpy as jnp
from jax import lax
from jax.experimental import pallas as pl
from jax.experimental.pallas import tpu as pltpu
from jax.sharding import PartitionSpec as P

MESH = pl.DeviceIdType.MESH
EPSILON = 0.5
F32 = jnp.float32
BF16 = jnp.bfloat16
NX, NY, NL, NH = 4, 4, 4, 4
NZ = NL * NH
CHIPS = NX * NY
D = 768
QS, TS = 32, 48
QB, TB = 2 * CHIPS * QS, NZ * TS
LOG2E = 1.4426950408889634
POT = EPSILON / LOG2E


def kernel(
    q_ref, t_ref, qm_ref, tm_ref,
    map_ref, qp_ref, tp_ref,
    qblk, tblk, tsib, plan, w, wsib, part, got, cols,
    rsend, rbuf, csend, cbuf, qmb, tms, tmb, fout, qpb, gout, tpb,
    q_send, q_recv, q_fwd, q_sib, t_send, t_recv, s_send, s_recv, ws_send, ws_recv,
    m_send, m_recv, r_send, r_recv, c_send, c_recv, o_send, o_recv, p_send, p_recv,
):
    row, col = lax.axis_index("row"), lax.axis_index("col")
    y, zh = row // NH, row % NH
    zl, x, core = col // (2 * NX), (col // 2) % NX, col % 2
    z = zh * NL + zl
    sib = 1 - core
    chip = y * NX + x
    mine = chip * 2 + core
    slot = zl * NH + zh

    def device(x_, y_, z_, core_):
        return (y_ * NH + z_ // NL, ((z_ % NL) * NX + x_) * 2 + core_)

    def group_peer(j):
        y_ = (y + j // (2 * NX)) % NY
        x_ = (x + (j // 2) % NX) % NX
        return device(x_, y_, z, (core + j) % 2)

    def chip_peer(j):
        return (x + j % NX) % NX, (y + j // NX) % NY

    def z_peer(j):
        return device(x, y, (z + j) % NZ, core)

    def send(src, dst, s_sem, r_sem, dev):
        pltpu.make_async_remote_copy(
            src_ref=src, dst_ref=dst, send_sem=s_sem, recv_sem=r_sem, device_id=dev, device_id_type=MESH
        ).start()

    def wait(ref, sem):
        pltpu.make_async_copy(ref, ref, sem).wait()

    barrier = pltpu.get_barrier_semaphore()

    @pl.loop(1, 2 * CHIPS)
    def _(j):
        pl.semaphore_signal(barrier, inc=1, device_id=group_peer(j), device_id_type=MESH)

    @pl.loop(1, NZ)
    def _(j):
        pl.semaphore_signal(barrier, inc=1, device_id=z_peer(j), device_id_type=MESH)

    tms_all = tm_ref[...]
    for i in range(NY):
        tms[i] = tms_all[:, i * NH * TS:(i + 1) * NH * TS]
    pl.semaphore_wait(barrier, 2 * CHIPS - 1 + NZ - 1)

    right, left = device(x, y, (z + 1) % NZ, core), device(x, y, (z + NZ - 1) % NZ, core)

    def t_slot(z_):
        return (z_ % NL) * NH + z_ // NL

    def t_copy(way, step, source):
        s = t_slot(source)
        src = t_ref if step == 0 else tblk.at[s]
        send(src, tblk.at[s], t_send.at[way], t_recv.at[way, step], right if way == 0 else left)

    t_copy(0, 0, z)
    t_copy(1, 0, z)

    @pl.loop(1, CHIPS)
    def _(j):
        x_, y_ = chip_peer(j)
        send(q_ref, qblk.at[mine], q_send, q_recv.at[chip], device(x_, y_, z, core))

    send(q_ref, qblk.at[mine], q_fwd, q_sib, device(x, y, z, sib))
    for j in range(1, NY):
        send(qm_ref.at[zl], qmb.at[y], m_send.at[0], m_recv.at[0], device(x, (y + j) % NY, z, core))
    for j in range(1, NL):
        send(tms.at[y], tmb.at[zl], m_send.at[1], m_recv.at[1], device(x, y, zh * NL + (zl + j) % NL, core))
    qblk[mine] = q_ref[...]
    tblk[slot] = t_ref[...]
    qmb[y] = qm_ref[zl]
    tmb[zl] = tms[y]

    STEPS = (NZ // 2, NZ // 2 - 1)
    for step in range(NZ // 2):
        for way in (0, 1):
            if step < STEPS[way]:
                source = (z - 1 - step + NZ) % NZ if way == 0 else (z + 1 + step) % NZ
                wait(tblk.at[t_slot(source)], t_recv.at[way, step])
                if step + 1 < STEPS[way]:
                    t_copy(way, step + 1, source)
        for j in range(1 + 2 * step, min(3 + 2 * step, CHIPS)):
            x_, y_ = (x + NX - j % NX) % NX, (y + NY - j // NX) % NY
            chip_ = y_ * NX + x_
            s = chip_ * 2 + core
            wait(qblk.at[s], q_recv.at[chip_])
            send(qblk.at[s], qblk.at[s], q_fwd, q_sib, device(x, y, z, sib))
    send(tblk, tsib, s_send, s_recv, device(x, y, z, sib))
    wait(qblk.at[pl.ds(0, CHIPS)], q_sib)

    wait(qmb.at[pl.ds(0, NY - 1)], m_recv.at[0])
    wait(tmb.at[pl.ds(0, NL - 1)], m_recv.at[1])
    lane = lax.broadcasted_iota(jnp.int32, (8, 128), 1)
    sub = lax.broadcasted_iota(jnp.int32, (8, 128), 0)
    mass_q = jnp.zeros((8, 128), F32)
    for b in range(8):
        line = qmb[b // 2, pl.ds(b % 2, 1), :]
        spread = jnp.broadcast_to(line, (128, 128)).T
        for k in range(16):
            mass_q = jnp.where(lane == b * 16 + k, spread[k * 8:k * 8 + 8, :], mass_q)
    mass_t = jnp.concatenate([tmb[i] for i in range(NL)], axis=1)

    def dense(v):
        out = jnp.zeros((8, 128), F32)
        for c in range(TB // 128):
            out = jnp.where(sub == c, v[:, c * 128:(c + 1) * 128], out)
        return out

    def undense(v):
        return jnp.concatenate([v[c:c + 1, :] for c in range(TB // 128)], axis=1)

    def gather_rows(n, value):
        rsend[n] = value
        rbuf[n, mine] = value

        @pl.loop(1, 2 * CHIPS)
        def _(j):
            send(rsend.at[n], rbuf.at[n, mine], r_send.at[n], r_recv.at[n], group_peer(j))

    def wait_rows(n):
        wait(rbuf.at[n, pl.ds(0, 2 * CHIPS - 1)], r_recv.at[n])
        return rbuf[n]

    def gather_cols(n, value):
        csend[n] = value
        cbuf[n, z] = value

        @pl.loop(1, NZ)
        def _(j):
            send(csend.at[n], cbuf.at[n, z], c_send.at[n], c_recv.at[n], z_peer(j))

    def wait_cols(n):
        wait(cbuf.at[n, pl.ds(0, NZ - 1)], c_recv.at[n])
        return cbuf[n]

    def lse(parts):
        top = jnp.max(parts, axis=0)
        return top + jnp.log2(jnp.sum(jnp.exp2(parts - top[None]), axis=0))

    RB = 64
    NB = QB // RB

    def pick(out, block, values):
        for g in range(RB // 8):
            out = jnp.where(lane == block * (RB // 8) + g, values[g * 8:(g + 1) * 8, :], out)
        return out

    def spread_rows(value):
        def body(b, v):
            for k in range(16):
                cols[pl.ds(pl.multiple_of(b * 128 + k * 8, 8), 8), :] = jnp.broadcast_to(v[:, k:k + 1], (8, 128))
            return pltpu.roll(v, 112, 1)
        lax.fori_loop(0, 8, body, value)

    def wide(r0, rows):
        return jnp.concatenate([cols[pl.ds(r0, rows), :]] * (TB // 128), axis=1)

    zero = jnp.zeros((8, 128), F32)

    scale = LOG2E / (EPSILON * math.sqrt(D))
    tools = tblk[...].reshape(TB, D)
    MB = 256

    def products(i, carry):
        a = qblk[pl.ds(i * (MB // QS), MB // QS)].reshape(MB, D)
        s = lax.dot_general(a, tools, (((1,), (1,)), ((), ())), preferred_element_type=F32)
        plan[pl.ds(pl.multiple_of(i * MB, MB), MB), :] = s * scale
        return carry

    lax.fori_loop(0, QB // MB, products, 0)

    def first_rows(i, carry):
        tops, sums = carry
        s = plan[pl.ds(pl.multiple_of(i * RB, RB), RB), :]
        top = jnp.max(s, axis=1, keepdims=True)
        total = jnp.sum(jnp.exp2(s - top), axis=1, keepdims=True)
        return pick(tops, i, top), pick(sums, i, total)

    tops, sums = lax.fori_loop(0, NB, first_rows, (zero, zero))
    gather_rows(0, tops + jnp.log2(sums))
    first_f = jnp.log2(mass_q) - lse(wait_rows(0))

    spread_rows(first_f)

    def col_max(i, top):
        r0 = pl.multiple_of(i * RB, RB)
        s = plan[pl.ds(r0, RB), :] + wide(r0, RB)
        plan[pl.ds(r0, RB), :] = s
        return jnp.maximum(top, jnp.max(s.reshape(RB // 8, 8, TB), axis=0))

    top8 = lax.fori_loop(0, NB, col_max, jnp.full((8, TB), -jnp.inf, F32))
    top = jnp.max(top8, axis=0, keepdims=True)

    def col_sum(i, acc):
        s = plan[pl.ds(pl.multiple_of(i * RB, RB), RB), :]
        return acc + jnp.sum(jnp.exp2(s - top).reshape(RB // 8, 8, TB), axis=0)

    acc = lax.fori_loop(0, NB, col_sum, jnp.zeros((8, TB), F32))
    gather_cols(0, dense(top + jnp.log2(jnp.sum(acc, axis=0, keepdims=True))))
    first_g = jnp.log2(mass_t) - undense(lse(wait_cols(0)))

    def second_rows(i, sums):
        r0 = pl.multiple_of(i * RB, RB)
        e = jnp.exp2(plan[pl.ds(r0, RB), :] + first_g)
        plan[pl.ds(r0, RB), :] = e
        return pick(sums, i, jnp.sum(e, axis=1, keepdims=True))

    def later_rows(v):
        def body(i, sums):
            e = plan[pl.ds(pl.multiple_of(i * RB, RB), RB), :] * v
            return pick(sums, i, jnp.sum(e, axis=1, keepdims=True))
        return lax.fori_loop(0, NB, body, zero)

    def later_cols():
        def body(i, acc):
            r0 = pl.multiple_of(i * RB, RB)
            e = plan[pl.ds(r0, RB), :] * wide(r0, RB)
            return acc + jnp.sum(e.reshape(RB // 8, 8, TB), axis=0)
        acc = lax.fori_loop(0, NB, body, jnp.zeros((8, TB), F32))
        return dense(jnp.sum(acc, axis=0, keepdims=True))

    gather_rows(1, lax.fori_loop(0, NB, second_rows, zero))
    u = mass_q / jnp.sum(wait_rows(1), axis=0)
    spread_rows(u)
    gather_cols(1, later_cols())
    v = mass_t / undense(jnp.sum(wait_cols(1), axis=0))
    gather_rows(2, later_rows(v))
    u = mass_q / jnp.sum(wait_rows(2), axis=0)
    spread_rows(u)
    gather_cols(2, later_cols())

    f = (first_f + jnp.log2(u)) * POT
    for b in range(8):
        block = jnp.concatenate(
            [jnp.broadcast_to(f[:, b * 16 + k:b * 16 + k + 1], (8, 128)) for k in range(16)], axis=0
        )
        fout[b // 2, pl.ds(b % 2, 1), :] = block.T[0:1, :]
    for j in range(1, NL):
        send(fout.at[y], qpb.at[zl], o_send.at[0], o_recv.at[0], device(x, y, zh * NL + (zl + j) % NL, core))
    qpb[zl] = fout[y]
    v = mass_t / undense(jnp.sum(wait_cols(2), axis=0))

    PB = 2 * QS

    def weights(i, sums):
        c = ((y + 1 + i // NX) % NY) * NX + i % NX
        r0 = pl.multiple_of(c * PB, PB)
        e = (plan[pl.ds(r0, PB), :] * wide(r0, PB) * v).astype(BF16)
        w[c] = e.reshape(2, QS, TB)
        return pick(sums, c, jnp.sum(e.astype(F32), axis=1, keepdims=True))

    wait(tsib, s_recv)
    sums = zero
    for h in range(NY):
        sums = lax.fori_loop(h * NX, (h + 1) * NX, weights, sums)
        y_ = (y + 1 + h) % NY
        send(w.at[pl.ds(y_ * NX, NX), sib], wsib.at[pl.ds(y_ * NX, NX)], ws_send, ws_recv.at[h], device(x, y, z, sib))
    gather_rows(3, sums)

    own, other = tools, tsib[...].reshape(TB, D)
    for h in range(NY):
        y_ = (y + 1 + h) % NY
        a = w[pl.ds(y_ * NX, NX), core].reshape(NX * QS, TB)
        p = jnp.dot(a, own, preferred_element_type=F32)
        wait(wsib.at[pl.ds(y_ * NX, NX)], ws_recv.at[h])
        b = wsib[pl.ds(y_ * NX, NX)].reshape(NX * QS, TB)
        p = p + jnp.dot(b, other, preferred_element_type=F32)
        part[pl.ds(y_ * NX, NX)] = p.reshape(NX, QS, D)
        for j in range(NX):
            x_ = (x + 1 + j) % NX
            if h < NY - 1 or j < NX - 1:
                send(part.at[y_ * NX + x_], got.at[chip], p_send, p_recv, device(x_, y_, z, core))

    g = (first_g + jnp.log2(v)) * POT
    for i in range(NL):
        gout[i] = g[:, i * NH * TS:(i + 1) * NH * TS]
    for j in range(1, NY):
        send(gout.at[zl], tpb.at[y], o_send.at[1], o_recv.at[1], device(x, (y + j) % NY, z, core))
    tpb[y] = gout[zl]
    wait(qpb.at[pl.ds(0, NL - 1)], o_recv.at[0])
    wait(tpb.at[pl.ds(0, NY - 1)], o_recv.at[1])
    qp_ref[...] = qpb[...]
    tp_ref[...] = jnp.concatenate([tpb[i] for i in range(NY)], axis=1)

    totals = jnp.sum(wait_rows(3), axis=0)
    spread_rows(totals)
    total = cols[pl.ds(pl.multiple_of(mine * QS, QS), QS), :]
    got[chip] = part[chip]
    wait(got.at[pl.ds(0, CHIPS - 1)], p_recv)
    full = jnp.sum(got[...], axis=0)
    map_ref[...] = (full / jnp.concatenate([total] * (D // 128), axis=1)).astype(BF16)

    wait(qblk.at[pl.ds(0, CHIPS - 1)], q_send)
    wait(qblk.at[pl.ds(0, CHIPS)], q_fwd)
    for way in (0, 1):
        wait(tblk.at[pl.ds(0, STEPS[way])], t_send.at[way])
    wait(tblk, s_send)
    wait(wsib, ws_send)
    wait(qmb.at[pl.ds(0, NY - 1)], m_send.at[0])
    wait(tmb.at[pl.ds(0, NL - 1)], m_send.at[1])
    wait(qpb.at[pl.ds(0, NL - 1)], o_send.at[0])
    wait(tpb.at[pl.ds(0, NY - 1)], o_send.at[1])
    for n in range(4):
        wait(rbuf.at[n, pl.ds(0, 2 * CHIPS - 1)], r_send.at[n])
    for n in range(3):
        wait(cbuf.at[n, pl.ds(0, NZ - 1)], c_send.at[n])
    wait(got.at[pl.ds(0, CHIPS - 1)], p_send)


def local(queries, tools, query_mass, tool_mass):
    vmem = pl.BlockSpec(memory_space=pltpu.VMEM)
    dma, V = pltpu.SemaphoreType.DMA, pltpu.VMEM
    mapped, qp, tp = pl.pallas_call(
        kernel,
        out_shape=(
            jax.ShapeDtypeStruct((QS, D), BF16),
            jax.ShapeDtypeStruct((NL, 2, 128), F32),
            jax.ShapeDtypeStruct((1, TB), F32),
        ),
        in_specs=[vmem] * 4,
        out_specs=(vmem,) * 3,
        scratch_shapes=[
            V((2 * CHIPS, QS, D), BF16), V((NZ, TS, D), BF16), V((NZ, TS, D), BF16), V((QB, TB), F32),
            V((CHIPS, 2, QS, TB), BF16), V((CHIPS, QS, TB), BF16), V((CHIPS, QS, D), F32), V((CHIPS, QS, D), F32),
            V((QB, 128), F32),
            V((4, 8, 128), F32), V((4, 2 * CHIPS, 8, 128), F32), V((3, 8, 128), F32), V((3, NZ, 8, 128), F32),
            V((NY, 2, 128), F32), V((NY, 1, NH * TS), F32), V((NL, 1, NH * TS), F32),
            V((NY, 2, 128), F32), V((NL, 2, 128), F32), V((NL, 1, NH * TS), F32), V((NY, 1, NH * TS), F32),
            dma, dma((CHIPS,)), dma, dma, dma((2,)), dma((2, NZ // 2)), dma, dma, dma, dma((NY,)),
            dma((2,)), dma((2,)), dma((4,)), dma((4,)), dma((3,)), dma((3,)), dma((2,)), dma((2,)), dma, dma,
        ],
        compiler_params=pltpu.CompilerParams(
            collective_id=0, has_side_effects=True, vmem_limit_bytes=48 * 1024 * 1024
        ),
    )(queries, tools, query_mass.reshape(NL, 2, 128), tool_mass.reshape(1, TB))
    return mapped, qp.reshape(QB), tp.reshape(TB)


def solution(mesh):
    in_specs = (P(("row", "col"), None), P(("col", "row"), None), P("row"), P("col"))
    out_specs = (P(("row", "col"), None), P("row"), P("col"))
    return jax.shard_map(local, mesh=mesh, in_specs=in_specs, out_specs=out_specs, check_vma=False)
```

```python
import math

import jax
import jax.numpy as jnp
from jax import lax
from jax.experimental import pallas as pl
from jax.experimental.pallas import tpu as pltpu
from jax.sharding import PartitionSpec as P

MESH = pl.DeviceIdType.MESH
EPSILON = 0.5
F32 = jnp.float32
BF16 = jnp.bfloat16
NX, NY, NL, NH = 4, 4, 4, 4
NZ = NL * NH
CHIPS = NX * NY
D = 768
QS, TS = 32, 48
QB, TB = 2 * CHIPS * QS, NZ * TS
LOG2E = 1.4426950408889634
POT = EPSILON / LOG2E


def kernel(
    q_hbm, t_hbm, qm_hbm, tm_hbm,
    map_ref, qp_ref, tp_ref,
    qblk, tblk, tsib, plan, w, wsib, part, got, cols,
    qm_ref, tm_ref, rsend, rbuf, csend, cbuf, qmb, tms, tmb, fout, qpb, gout, tpb,
    l_sem, q_send, q_recv, q_fwd, q_sib, t_send, t_recv, s_send, s_recv, ws_send, ws_recv,
    m_send, m_recv, r_send, r_recv, c_send, c_recv, o_send, o_recv, p_send, p_recv,
):
    row, col = lax.axis_index("row"), lax.axis_index("col")
    y, zh = row // NH, row % NH
    zl, x, core = col // (2 * NX), (col // 2) % NX, col % 2
    z = zh * NL + zl
    sib = 1 - core
    chip = y * NX + x
    mine = chip * 2 + core
    slot = zl * NH + zh

    def device(x_, y_, z_, core_):
        return (y_ * NH + z_ // NL, ((z_ % NL) * NX + x_) * 2 + core_)

    def far(j, n):
        return (n // 2 + ((j + 1) // 2) * (1 - 2 * (j % 2)) + n) % n

    def group_peer(j):
        y_ = (y + far(j // (2 * NX), NY)) % NY
        x_ = (x + far((j // 2) % NX, NX)) % NX
        return device(x_, y_, z, (core + 1 + j) % 2)

    def chip_peer(j):
        return (x + j % NX) % NX, (y + j // NX) % NY

    def z_peer(j):
        return device(x, y, (z + far(j, NZ)) % NZ, core)

    def send(src, dst, s_sem, r_sem, dev):
        pltpu.make_async_remote_copy(
            src_ref=src, dst_ref=dst, send_sem=s_sem, recv_sem=r_sem, device_id=dev, device_id_type=MESH
        ).start()

    def wait(ref, sem):
        pltpu.make_async_copy(ref, ref, sem).wait()

    barrier = pltpu.get_barrier_semaphore()
    for near in (2, NZ - 2, 1, NZ - 1):
        peer = device(x, y, (z + near) % NZ, core)
        pl.semaphore_signal(barrier, inc=1, device_id=peer, device_id_type=MESH)

    @pl.loop(0, 2 * CHIPS - 1)
    def _(j):
        pl.semaphore_signal(barrier, inc=1, device_id=group_peer(j), device_id_type=MESH)

    loads = [
        pltpu.make_async_copy(t_hbm, tblk.at[slot], l_sem.at[0]),
        pltpu.make_async_copy(q_hbm, qblk.at[mine], l_sem.at[1]),
        pltpu.make_async_copy(qm_hbm, qm_ref, l_sem.at[2]),
        pltpu.make_async_copy(tm_hbm, tm_ref, l_sem.at[3]),
    ]
    for load in loads:
        load.start()
    for load in loads:
        load.wait()
    tms_all = jnp.concatenate([tm_ref[c:c + 1, :] for c in range(TB // 128)], axis=1)
    for i in range(NY):
        tms[i] = tms_all[:, i * NH * TS:(i + 1) * NH * TS]
    pl.semaphore_wait(barrier, 2 * CHIPS - 1 + 4)

    lane = lax.broadcasted_iota(jnp.int32, (8, 128), 1)
    zero = jnp.zeros((8, 128), F32)
    RB = 64
    NB = QB // RB

    def pick(out, block, values):
        n = values.shape[0] // 8
        for g in range(n):
            out = jnp.where(lane == block * n + g, values[g * 8:(g + 1) * 8, :], out)
        return out

    scale = LOG2E / (EPSILON * math.sqrt(D))
    HB, MB = TB // 2, 256

    def products(half):
        lanes = pl.ds(pl.multiple_of(half * HB, 128), HB)
        tools = tblk[pl.ds(half * (NZ // 2), NZ // 2)].reshape(HB, D)

        def body(i, carry):
            tops, sums = carry
            a = qblk[pl.ds(i * (MB // QS), MB // QS)].reshape(MB, D)
            s = scale * lax.dot_general(a, tools, (((1,), (1,)), ((), ())), preferred_element_type=F32)
            plan[pl.ds(pl.multiple_of(i * MB, MB), MB), lanes] = s
            top = jnp.max(s, axis=1, keepdims=True)
            total = jnp.sum(jnp.exp2(s - top), axis=1, keepdims=True)
            return pick(tops, i, top), pick(sums, i, total)

        return lax.fori_loop(0, QB // MB, body, (zero, zero))

    def t_slot(z_):
        return (z_ % NL) * NH + z_ // NL

    PIECES, PIECE = 3, TS // 3

    def t_piece(source, p):
        return tblk.at[t_slot(source), pl.ds(p * PIECE, PIECE)]

    REACH = (NZ // 2, NZ // 2 - 1)

    def t_source(way, dist):
        return (z + NZ - dist) % NZ if way == 0 else (z + dist) % NZ

    def t_forward(way, dist, p):
        piece = t_piece(t_source(way, dist), p)
        for hop in (2, 1):
            if dist % 2 == 0 and dist + hop <= REACH[way]:
                to = device(x, y, t_source(way, NZ - hop), core)
                send(piece, piece, t_send.at[way], t_recv.at[way, dist + hop - 1, p], to)

    for p in range(PIECES):
        for way in (0, 1):
            t_forward(way, 0, p)

    @pl.loop(1, CHIPS)
    def _(j):
        x_, y_ = chip_peer(j)
        send(qblk.at[mine], qblk.at[mine], q_send, q_recv.at[chip], device(x_, y_, z, core))

    send(qblk.at[mine], qblk.at[mine], q_fwd, q_sib, device(x, y, z, sib))
    for j in range(1, NY):
        send(qm_ref.at[zl], qmb.at[y], m_send.at[0], m_recv.at[0], device(x, (y + j) % NY, z, core))
    qmb[y] = qm_ref[zl]
    tmb[zl] = tms[y]

    for step, dist in enumerate((2, 1, 4, 3, 6, 5, 7, 8)):
        for p in range(PIECES):
            for way in (0, 1):
                if dist <= REACH[way]:
                    wait(t_piece(t_source(way, dist), p), t_recv.at[way, dist - 1, p])
                    t_forward(way, dist, p)
        for j in range(1 + 3 * (step - 2), min(4 + 3 * (step - 2), CHIPS)):
            if j < 1:
                continue
            x_, y_ = (x + NX - j % NX) % NX, (y + NY - j // NX) % NY
            chip_ = y_ * NX + x_
            s = chip_ * 2 + core
            wait(qblk.at[s], q_recv.at[chip_])
            send(qblk.at[s], qblk.at[s], q_fwd, q_sib, device(x, y, z, sib))
        if step == NL - 1:
            for j in range(1, NL):
                send(tms.at[y], tmb.at[zl], m_send.at[1], m_recv.at[1], device(x, y, zh * NL + (zl + j) % NL, core))
        if step == NZ // 2 - 2:
            wait(qblk.at[pl.ds(0, CHIPS)], q_sib)
            early = products(1 - zl // 2)
    send(tblk, tsib, s_send, s_recv, device(x, y, z, sib))

    wait(qmb.at[pl.ds(0, NY - 1)], m_recv.at[0])
    wait(tmb.at[pl.ds(0, NL - 1)], m_recv.at[1])
    mass_q = jnp.zeros((8, 128), F32)
    for b in range(8):
        line = qmb[b // 2, pl.ds(b % 2, 1), :]
        spread = jnp.broadcast_to(line, (128, 128)).T
        for k in range(16):
            mass_q = jnp.where(lane == b * 16 + k, spread[k * 8:k * 8 + 8, :], mass_q)
    mass_t = jnp.concatenate([tmb[i] for i in range(NL)], axis=1)

    def dense(v):
        return jnp.concatenate([v[:, c * 128:(c + 1) * 128] for c in range(TB // 128)], axis=0)

    def undense(v):
        return jnp.concatenate([v[c:c + 1, :] for c in range(TB // 128)], axis=1)

    def gather_rows(n, value):
        rsend[n] = value
        rbuf[n, mine] = value

        @pl.loop(0, 2 * CHIPS - 1)
        def _(j):
            send(rsend.at[n], rbuf.at[n, mine], r_send.at[n], r_recv.at[n], group_peer(j))

    def wait_rows(n):
        wait(rbuf.at[n, pl.ds(0, 2 * CHIPS - 1)], r_recv.at[n])
        return rbuf[n]

    def gather_cols(n, value):
        csend[n] = value
        cbuf[n, z] = value

        @pl.loop(0, NZ - 1)
        def _(j):
            send(csend.at[n], cbuf.at[n, z], c_send.at[n], c_recv.at[n], z_peer(j))

    def wait_cols(n):
        wait(cbuf.at[n, pl.ds(0, NZ - 1)], c_recv.at[n])
        return cbuf[n]

    def lse(parts):
        top = jnp.max(parts, axis=0)
        return top + jnp.log2(jnp.sum(jnp.exp2(parts - top[None]), axis=0))

    def spread_rows(value):
        def body(b, v):
            for k in range(16):
                cols[pl.ds(pl.multiple_of(b * 128 + k * 8, 8), 8), :] = jnp.broadcast_to(v[:, k:k + 1], (8, 128))
            return pltpu.roll(v, 112, 1)
        lax.fori_loop(0, 8, body, value)

    def wide(r0, rows):
        return jnp.concatenate([cols[pl.ds(r0, rows), :]] * (TB // 128), axis=1)

    (top_a, sum_a), (top_b, sum_b) = early, products(zl // 2)
    tops = jnp.maximum(top_a, top_b)
    sums = sum_a * jnp.exp2(top_a - tops) + sum_b * jnp.exp2(top_b - tops)
    gather_rows(0, tops + jnp.log2(sums))
    first_f = jnp.log2(mass_q) - lse(wait_rows(0))

    spread_rows(first_f)

    def col_max(i, top):
        r0 = pl.multiple_of(i * RB, RB)
        s = plan[pl.ds(r0, RB), :] + wide(r0, RB)
        plan[pl.ds(r0, RB), :] = s
        return jnp.maximum(top, jnp.max(s.reshape(RB // 8, 8, TB), axis=0))

    top8 = lax.fori_loop(0, NB, col_max, jnp.full((8, TB), -jnp.inf, F32))
    top = jnp.max(top8, axis=0, keepdims=True)

    def col_sum(i, acc):
        s = plan[pl.ds(pl.multiple_of(i * RB, RB), RB), :]
        return acc + jnp.sum(jnp.exp2(s - top).reshape(RB // 8, 8, TB), axis=0)

    acc = lax.fori_loop(0, NB, col_sum, jnp.zeros((8, TB), F32))
    gather_cols(0, dense(top + jnp.log2(jnp.sum(acc, axis=0, keepdims=True))))
    first_g = jnp.log2(mass_t) - undense(lse(wait_cols(0)))

    def second_rows(i, sums):
        r0 = pl.multiple_of(i * RB, RB)
        e = jnp.exp2(plan[pl.ds(r0, RB), :] + first_g)
        plan[pl.ds(r0, RB), :] = e
        return pick(sums, i, jnp.sum(e, axis=1, keepdims=True))

    def later_rows(v):
        def body(i, sums):
            e = plan[pl.ds(pl.multiple_of(i * RB, RB), RB), :] * v
            return pick(sums, i, jnp.sum(e, axis=1, keepdims=True))
        return lax.fori_loop(0, NB, body, zero)

    def later_cols():
        def body(i, acc):
            r0 = pl.multiple_of(i * RB, RB)
            e = plan[pl.ds(r0, RB), :] * wide(r0, RB)
            return acc + jnp.sum(e.reshape(RB // 8, 8, TB), axis=0)
        acc = lax.fori_loop(0, NB, body, jnp.zeros((8, TB), F32))
        return dense(jnp.sum(acc, axis=0, keepdims=True))

    gather_rows(1, lax.fori_loop(0, NB, second_rows, zero))
    u = mass_q / jnp.sum(wait_rows(1), axis=0)
    spread_rows(u)
    gather_cols(1, later_cols())
    v = mass_t / undense(jnp.sum(wait_cols(1), axis=0))
    gather_rows(2, later_rows(v))
    u = mass_q / jnp.sum(wait_rows(2), axis=0)
    spread_rows(u)
    gather_cols(2, later_cols())

    f = (first_f + jnp.log2(u)) * POT
    for b in range(8):
        block = jnp.concatenate(
            [jnp.broadcast_to(f[:, b * 16 + k:b * 16 + k + 1], (8, 128)) for k in range(16)], axis=0
        )
        fout[b // 2, pl.ds(b % 2, 1), :] = block.T[0:1, :]
    for j in range(1, NL):
        send(fout.at[y], qpb.at[zl], o_send.at[0], o_recv.at[0], device(x, y, zh * NL + (zl + j) % NL, core))
    qpb[zl] = fout[y]
    v = mass_t / undense(jnp.sum(wait_cols(2), axis=0))

    PB = 2 * QS

    def weights(i, sums):
        c = ((y + 1 + i // NX) % NY) * NX + i % NX
        r0 = pl.multiple_of(c * PB, PB)
        e = (plan[pl.ds(r0, PB), :] * wide(r0, PB) * v).astype(BF16)
        w[c] = e.reshape(2, QS, TB)
        return pick(sums, c, jnp.sum(e.astype(F32), axis=1, keepdims=True))

    wait(tsib, s_recv)
    sums = zero
    for h in range(NY):
        sums = lax.fori_loop(h * NX, (h + 1) * NX, weights, sums)
        y_ = (y + 1 + h) % NY
        send(w.at[pl.ds(y_ * NX, NX), sib], wsib.at[pl.ds(y_ * NX, NX)], ws_send, ws_recv.at[h], device(x, y, z, sib))
    gather_rows(3, sums)

    own, other = tblk[...].reshape(TB, D), tsib[...].reshape(TB, D)
    for h in range(NY):
        y_ = (y + 1 + h) % NY
        a = w[pl.ds(y_ * NX, NX), core].reshape(NX * QS, TB)
        p = jnp.dot(a, own, preferred_element_type=F32)
        wait(wsib.at[pl.ds(y_ * NX, NX)], ws_recv.at[h])
        b = wsib[pl.ds(y_ * NX, NX)].reshape(NX * QS, TB)
        p = p + jnp.dot(b, other, preferred_element_type=F32)
        part[pl.ds(y_ * NX, NX)] = p.reshape(NX, QS, D)
        for j in range(NX):
            x_ = (x + 1 + j) % NX
            if h < NY - 1 or j < NX - 1:
                send(part.at[y_ * NX + x_], got.at[chip], p_send, p_recv, device(x_, y_, z, core))

    g = (first_g + jnp.log2(v)) * POT
    for i in range(NL):
        gout[i] = g[:, i * NH * TS:(i + 1) * NH * TS]
    for j in range(1, NY):
        send(gout.at[zl], tpb.at[y], o_send.at[1], o_recv.at[1], device(x, (y + j) % NY, z, core))
    tpb[y] = gout[zl]
    wait(qpb.at[pl.ds(0, NL - 1)], o_recv.at[0])
    wait(tpb.at[pl.ds(0, NY - 1)], o_recv.at[1])
    qp_ref[...] = qpb[...]
    tp_ref[...] = dense(jnp.concatenate([tpb[i] for i in range(NY)], axis=1))

    totals = jnp.sum(wait_rows(3), axis=0)
    spread_rows(totals)
    total = cols[pl.ds(pl.multiple_of(mine * QS, QS), QS), :]
    got[chip] = part[chip]
    wait(got.at[pl.ds(0, CHIPS - 1)], p_recv)
    full = jnp.sum(got[...], axis=0)
    map_ref[...] = (full / jnp.concatenate([total] * (D // 128), axis=1)).astype(BF16)

    wait(qblk.at[pl.ds(0, CHIPS - 1)], q_send)
    wait(qblk.at[pl.ds(0, CHIPS)], q_fwd)
    for way in (0, 1):
        wait(tblk.at[pl.ds(0, REACH[way])], t_send.at[way])
    wait(tblk, s_send)
    wait(wsib, ws_send)
    wait(qmb.at[pl.ds(0, NY - 1)], m_send.at[0])
    wait(tmb.at[pl.ds(0, NL - 1)], m_send.at[1])
    wait(qpb.at[pl.ds(0, NL - 1)], o_send.at[0])
    wait(tpb.at[pl.ds(0, NY - 1)], o_send.at[1])
    for n in range(4):
        wait(rbuf.at[n, pl.ds(0, 2 * CHIPS - 1)], r_send.at[n])
    for n in range(3):
        wait(cbuf.at[n, pl.ds(0, NZ - 1)], c_send.at[n])
    wait(got.at[pl.ds(0, CHIPS - 1)], p_send)


def local(queries, tools, query_mass, tool_mass):
    vmem = pl.BlockSpec(memory_space=pltpu.VMEM)
    dma, V = pltpu.SemaphoreType.DMA, pltpu.VMEM
    mapped, qp, tp = pl.pallas_call(
        kernel,
        out_shape=(
            jax.ShapeDtypeStruct((QS, D), BF16),
            jax.ShapeDtypeStruct((NL, 2, 128), F32),
            jax.ShapeDtypeStruct((TB // 128, 128), F32),
        ),
        in_specs=[pl.BlockSpec(memory_space=pltpu.HBM)] * 4,
        out_specs=(vmem,) * 3,
        scratch_shapes=[
            V((2 * CHIPS, QS, D), BF16), V((NZ, TS, D), BF16), V((NZ, TS, D), BF16), V((QB, TB), F32),
            V((CHIPS, 2, QS, TB), BF16), V((CHIPS, QS, TB), BF16), V((CHIPS, QS, D), F32), V((CHIPS, QS, D), F32),
            V((QB, 128), F32),
            V((NL, 2, 128), F32), V((TB // 128, 128), F32),
            V((4, 8, 128), F32), V((4, 2 * CHIPS, 8, 128), F32), V((3, TB // 128, 128), F32), V((3, NZ, TB // 128, 128), F32),
            V((NY, 2, 128), F32), V((NY, 1, NH * TS), F32), V((NL, 1, NH * TS), F32),
            V((NY, 2, 128), F32), V((NL, 2, 128), F32), V((NL, 1, NH * TS), F32), V((NY, 1, NH * TS), F32),
            dma((4,)), dma, dma((CHIPS,)), dma, dma, dma((2,)), dma((2, NZ // 2, 3)), dma, dma, dma, dma((NY,)),
            dma((2,)), dma((2,)), dma((4,)), dma((4,)), dma((3,)), dma((3,)), dma((2,)), dma((2,)), dma, dma,
        ],
        compiler_params=pltpu.CompilerParams(
            collective_id=0, has_side_effects=True, vmem_limit_bytes=60 * 1024 * 1024
        ),
    )(queries, tools, query_mass.reshape(NL, 2, 128), tool_mass.reshape(TB // 128, 128))
    return mapped, qp.reshape(QB), tp.reshape(TB)


def solution(mesh):
    in_specs = (P(("row", "col"), None), P(("col", "row"), None), P("row"), P("col"))
    out_specs = (P(("row", "col"), None), P("row"), P("col"))
    return jax.shard_map(local, mesh=mesh, in_specs=in_specs, out_specs=out_specs, check_vma=False)
```

```python
import functools
import math

import jax
import jax.numpy as jnp
from jax import lax
from jax.experimental import pallas as pl
from jax.experimental.pallas import tpu as pltpu
from jax.sharding import PartitionSpec as P

MESH = pl.DeviceIdType.MESH
EPSILON = 0.5
F32 = jnp.float32
BF16 = jnp.bfloat16
NX, NY, NL, NH = 4, 4, 4, 4
NZ = NL * NH
CHIPS = NX * NY
D = 768
QS, TS = 32, 48
QB, TB = 2 * CHIPS * QS, NZ * TS
LOG2E = 1.4426950408889634
POT = EPSILON / LOG2E


def kernel(
    q_hbm, t_hbm, qm_hbm, tm_hbm,
    map_ref, qp_ref, tp_ref,
    qblk, tblk, tsib, plan, w, wsib, part, got, half, last, cols,
    qm_ref, tm_ref, rsend, rbuf, csend, cbuf, qmb, tms, tmb, fout, qpb, gout, tpb,
    l_sem, q_send, q_recv, q_fwd, q_sib, t_send, t_recv, s_send, s_recv, ws_send, ws_recv,
    m_send, m_recv, r_send, r_recv, c_send, c_recv, o_send, o_recv, p_send, p_recv, h_send, h_recv,
):
    row, col = lax.axis_index("row"), lax.axis_index("col")
    y, zh = row // NH, row % NH
    zl, x, core = col // (2 * NX), (col // 2) % NX, col % 2
    z = zh * NL + zl
    sib = 1 - core
    chip = y * NX + x
    mine = chip * 2 + core
    slot = zl * NH + zh

    def device(x_, y_, z_, core_):
        return (y_ * NH + z_ // NL, ((z_ % NL) * NX + x_) * 2 + core_)

    def far(j, n):
        return (n // 2 + ((j + 1) // 2) * (1 - 2 * (j % 2)) + n) % n

    def group_peer(j):
        y_ = (y + far(j // (2 * NX), NY)) % NY
        x_ = (x + far((j // 2) % NX, NX)) % NX
        return device(x_, y_, z, (core + 1 + j) % 2)

    def z_peer(j):
        return device(x, y, (z + far(j, NZ)) % NZ, core)

    def send(src, dst, s_sem, r_sem, dev):
        pltpu.make_async_remote_copy(
            src_ref=src, dst_ref=dst, send_sem=s_sem, recv_sem=r_sem, device_id=dev, device_id_type=MESH
        ).start()

    def wait(ref, sem):
        pltpu.make_async_copy(ref, ref, sem).wait()

    barrier = pltpu.get_barrier_semaphore()
    for near in (2, NZ - 2, 1, NZ - 1):
        peer = device(x, y, (z + near) % NZ, core)
        pl.semaphore_signal(barrier, inc=1, device_id=peer, device_id_type=MESH)

    hops = {0: 0, 1: 1, 2: 2, 3: 1}
    shifts = [(a, b) for a in (2, 1, 3, 0) for b in (2, 1, 3, 0) if (a, b) != (0, 0)]
    near_chips = [s for s in shifts if hops[s[0]] + hops[s[1]] <= 2]
    far_chips = [s for s in shifts if s not in near_chips]
    for a, b in near_chips + [(0, 0)]:
        for core_ in (sib, core) if (a, b) != (0, 0) else (sib,):
            peer = device((x + a) % NX, (y + b) % NY, z, core_)
            pl.semaphore_signal(barrier, inc=1, device_id=peer, device_id_type=MESH)

    loads = [
        pltpu.make_async_copy(t_hbm, tblk.at[slot], l_sem.at[0]),
        pltpu.make_async_copy(q_hbm, qblk.at[mine], l_sem.at[1]),
        pltpu.make_async_copy(qm_hbm, qm_ref, l_sem.at[2]),
        pltpu.make_async_copy(tm_hbm, tm_ref, l_sem.at[3]),
    ]
    for load in loads:
        load.start()
    for load in loads:
        load.wait()
    tms_all = jnp.concatenate([tm_ref[c:c + 1, :] for c in range(TB // 128)], axis=1)
    for i in range(NY):
        tms[i] = tms_all[:, i * NH * TS:(i + 1) * NH * TS]
    pl.semaphore_wait(barrier, 2 * len(near_chips) + 1 + 4)

    lane = lax.broadcasted_iota(jnp.int32, (8, 128), 1)
    zero = jnp.zeros((8, 128), F32)
    RB = 64
    NB = QB // RB

    def pick(out, block, values):
        n = values.shape[0] // 8
        for g in range(n):
            out = jnp.where(lane == block * n + g, values[g * 8:(g + 1) * 8, :], out)
        return out

    scale = LOG2E / (EPSILON * math.sqrt(D))
    HB, MB = TB // 2, 256

    def products(half):
        lanes = pl.ds(pl.multiple_of(half * HB, 128), HB)
        tools = tblk[pl.ds(half * (NZ // 2), NZ // 2)].reshape(HB, D)

        def body(i, carry):
            tops, sums = carry
            a = qblk[pl.ds(i * (MB // QS), MB // QS)].reshape(MB, D)
            s = scale * lax.dot_general(a, tools, (((1,), (1,)), ((), ())), preferred_element_type=F32)
            plan[pl.ds(pl.multiple_of(i * MB, MB), MB), lanes] = s
            top = jnp.max(s, axis=1, keepdims=True)
            total = jnp.sum(jnp.exp2(s - top), axis=1, keepdims=True)
            return pick(tops, i, top), pick(sums, i, total)

        return lax.fori_loop(0, QB // MB, body, (zero, zero))

    def t_slot(z_):
        return (z_ % NL) * NH + z_ // NL

    PIECES, PIECE = 3, TS // 3

    def t_piece(source, p):
        return tblk.at[t_slot(source), pl.ds(p * PIECE, PIECE)]

    def reach(way, p):
        return NZ // 2 if (way == 0) == (p < 2) else NZ // 2 - 1

    def t_source(way, dist):
        return (z + NZ - dist) % NZ if way == 0 else (z + dist) % NZ

    ONWARD = {0: (2, 1), 2: (4, 3), 4: (5,), 5: (6,), 6: (7,), 7: (8,)}

    def t_forward(way, dist, p):
        piece = t_piece(t_source(way, dist), p)
        for there in ONWARD.get(dist, ()):
            if there <= reach(way, p):
                to = device(x, y, t_source(way, NZ + dist - there), core)
                send(piece, piece, t_send.at[way], t_recv.at[way, there - 1, p], to)

    for p in range(PIECES):
        for way in (0, 1):
            t_forward(way, 0, p)

    def q_give(a, b):
        to = device((x + a) % NX, (y + b) % NY, z, core)
        send(qblk.at[mine], qblk.at[mine], q_send, q_recv.at[chip], to)

    def q_take(a, b):
        chip_ = ((y + b) % NY) * NX + (x + a) % NX
        s = chip_ * 2 + core
        wait(qblk.at[s], q_recv.at[chip_])
        send(qblk.at[s], qblk.at[s], q_fwd, q_sib, device(x, y, z, sib))

    for a, b in near_chips:
        q_give(a, b)
    corners = [(1, 1), (3, 1), (1, 3)]
    others = [s for s in near_chips if s not in corners] + far_chips
    send(qblk.at[mine], qblk.at[mine], q_fwd, q_sib, device(x, y, z, sib))
    for j in range(1, NY):
        send(qm_ref.at[zl], qmb.at[y], m_send.at[0], m_recv.at[0], device(x, (y + j) % NY, z, core))
    qmb[y] = qm_ref[zl]
    tmb[zl] = tms[y]

    for step, dist in enumerate((2, 1, 4, 3, 5, 6, 7, 8)):
        for p in range(PIECES):
            for way in (0, 1):
                if dist <= reach(way, p):
                    wait(t_piece(t_source(way, dist), p), t_recv.at[way, dist - 1, p])
                    t_forward(way, dist, p)
        if step == 1:
            for a, b in corners:
                q_take(a, b)
            for a, b in far_chips:
                q_give(a, b)
        if 3 <= step < 7:
            for a, b in others[3 * (step - 3):3 * (step - 2)]:
                q_take(a, b)
        if step == NL - 1:
            for j in range(1, NL):
                send(tms.at[y], tmb.at[zl], m_send.at[1], m_recv.at[1], device(x, y, zh * NL + (zl + j) % NL, core))
        if step == NZ // 2 - 2:
            wait(qblk.at[pl.ds(0, CHIPS)], q_sib)
            early = products(1 - zl // 2)
    send(tblk, tsib, s_send, s_recv, device(x, y, z, sib))

    wait(qmb.at[pl.ds(0, NY - 1)], m_recv.at[0])
    wait(tmb.at[pl.ds(0, NL - 1)], m_recv.at[1])
    mass_q = jnp.zeros((8, 128), F32)
    for b in range(8):
        line = qmb[b // 2, pl.ds(b % 2, 1), :]
        spread = jnp.broadcast_to(line, (128, 128)).T
        for k in range(16):
            mass_q = jnp.where(lane == b * 16 + k, spread[k * 8:k * 8 + 8, :], mass_q)
    mass_t = jnp.concatenate([tmb[i] for i in range(NL)], axis=1)

    def dense(v):
        return jnp.concatenate([v[:, c * 128:(c + 1) * 128] for c in range(TB // 128)], axis=0)

    def undense(v):
        return jnp.concatenate([v[c:c + 1, :] for c in range(TB // 128)], axis=1)

    def gather_rows(n, value):
        rsend[n] = value
        rbuf[n, mine] = value

        @pl.loop(0, 2 * CHIPS - 1)
        def _(j):
            send(rsend.at[n], rbuf.at[n, mine], r_send.at[n], r_recv.at[n], group_peer(j))

    def wait_rows(n):
        wait(rbuf.at[n, pl.ds(0, 2 * CHIPS - 1)], r_recv.at[n])
        return rbuf[n]

    def gather_cols(n, value):
        csend[n] = value
        cbuf[n, z] = value

        @pl.loop(0, NZ - 1)
        def _(j):
            send(csend.at[n], cbuf.at[n, z], c_send.at[n], c_recv.at[n], z_peer(j))

    def wait_cols(n):
        wait(cbuf.at[n, pl.ds(0, NZ - 1)], c_recv.at[n])
        return cbuf[n]

    def lse(parts):
        top = jnp.max(parts, axis=0)
        return top + jnp.log2(jnp.sum(jnp.exp2(parts - top[None]), axis=0))

    def spread_rows(value):
        for k in range(QB // 8):
            cols[k * 8:k * 8 + 8, :] = jnp.broadcast_to(value[:, k:k + 1], (8, 128))

    def wide(r0, rows):
        return jnp.concatenate([cols[pl.ds(r0, rows), :]] * (TB // 128), axis=1)

    (top_a, sum_a), (top_b, sum_b) = early, products(zl // 2)
    tops = jnp.maximum(top_a, top_b)
    sums = sum_a * jnp.exp2(top_a - tops) + sum_b * jnp.exp2(top_b - tops)
    gather_rows(0, tops + jnp.log2(sums))
    first_f = jnp.log2(mass_q) - lse(wait_rows(0))

    spread_rows(first_f)

    def col_max(i, top):
        r0 = pl.multiple_of(i * RB, RB)
        s = plan[pl.ds(r0, RB), :] + wide(r0, RB)
        plan[pl.ds(r0, RB), :] = s
        return jnp.maximum(top, jnp.max(s.reshape(RB // 8, 8, TB), axis=0))

    top8 = lax.fori_loop(0, NB, col_max, jnp.full((8, TB), -jnp.inf, F32))
    top = jnp.max(top8, axis=0, keepdims=True)

    def col_sum(i, acc):
        s = plan[pl.ds(pl.multiple_of(i * RB, RB), RB), :]
        return acc + jnp.sum(jnp.exp2(s - top).reshape(RB // 8, 8, TB), axis=0)

    acc = lax.fori_loop(0, NB, col_sum, jnp.zeros((8, TB), F32))
    gather_cols(0, dense(top + jnp.log2(jnp.sum(acc, axis=0, keepdims=True))))
    first_g = jnp.log2(mass_t) - undense(lse(wait_cols(0)))

    def second_rows(i, sums):
        r0 = pl.multiple_of(i * RB, RB)
        e = jnp.exp2(plan[pl.ds(r0, RB), :] + first_g)
        plan[pl.ds(r0, RB), :] = e
        return pick(sums, i, jnp.sum(e, axis=1, keepdims=True))

    def later_rows(v):
        def body(i, sums):
            e = plan[pl.ds(pl.multiple_of(i * RB, RB), RB), :] * v
            return pick(sums, i, jnp.sum(e, axis=1, keepdims=True))
        return lax.fori_loop(0, NB, body, zero)

    def later_cols():
        def body(i, acc):
            r0 = pl.multiple_of(i * RB, RB)
            e = plan[pl.ds(r0, RB), :] * wide(r0, RB)
            return acc + jnp.sum(e.reshape(RB // 8, 8, TB), axis=0)
        acc = lax.fori_loop(0, NB, body, jnp.zeros((8, TB), F32))
        return dense(jnp.sum(acc, axis=0, keepdims=True))

    gather_rows(1, lax.fori_loop(0, NB, second_rows, zero))
    u = mass_q / jnp.sum(wait_rows(1), axis=0)
    spread_rows(u)
    gather_cols(1, later_cols())
    v = mass_t / undense(jnp.sum(wait_cols(1), axis=0))
    gather_rows(2, later_rows(v))
    u = mass_q / jnp.sum(wait_rows(2), axis=0)
    spread_rows(u)
    gather_cols(2, later_cols())

    f = (first_f + jnp.log2(u)) * POT
    for b in range(8):
        block = jnp.concatenate(
            [jnp.broadcast_to(f[:, b * 16 + k:b * 16 + k + 1], (8, 128)) for k in range(16)], axis=0
        )
        fout[b // 2, pl.ds(b % 2, 1), :] = block.T[0:1, :]
    for j in range(1, NL):
        send(fout.at[y], qpb.at[zl], o_send.at[0], o_recv.at[0], device(x, y, zh * NL + (zl + j) % NL, core))
    qpb[zl] = fout[y]
    v = mass_t / undense(jnp.sum(wait_cols(2), axis=0))

    PB = 2 * QS

    def weights(y_, i, sums):
        c = y_ * NX + i
        r0 = pl.multiple_of(c * PB, PB)
        e = (plan[pl.ds(r0, PB), :] * wide(r0, PB) * v).astype(BF16)
        w[c] = e.reshape(2, QS, TB)
        return pick(sums, c, jnp.sum(e.astype(F32), axis=1, keepdims=True))

    wait(tsib, s_recv)
    sums = zero
    for h in range(NY):
        y_ = (y + (2, 1, 3, 0)[h]) % NY
        sums = lax.fori_loop(0, NX, functools.partial(weights, y_), sums)
        send(w.at[pl.ds(y_ * NX, NX), sib], wsib.at[pl.ds(y_ * NX, NX)], ws_send, ws_recv.at[h], device(x, y, z, sib))
    gather_rows(3, sums)

    own, other = tblk[...].reshape(TB, D), tsib[...].reshape(TB, D)
    HD = D // 2
    for h, dy in enumerate((2, 1, 3, 0)):
        y_ = (y + dy) % NY
        a = w[pl.ds(y_ * NX, NX), core].reshape(NX * QS, TB)
        p = jnp.dot(a, own, preferred_element_type=F32)
        wait(wsib.at[pl.ds(y_ * NX, NX)], ws_recv.at[h])
        b = wsib[pl.ds(y_ * NX, NX)].reshape(NX * QS, TB)
        p = p + jnp.dot(b, other, preferred_element_type=F32)
        for f in (0, 1):
            part[f, pl.ds(y_ * NX, NX)] = p[:, f * HD:(f + 1) * HD].reshape(NX, QS, HD)
        for dx in (2, 1, 3, 0):
            x_ = (x + dx) % NX
            if dx:
                send(part.at[0, y_ * NX + x_], got.at[0, y_, x], p_send.at[0], p_recv.at[0, y_], device(x_, y, z, core))
            else:
                got[0, y_, x] = part[0, y_ * NX + x]
            if dy:
                send(part.at[1, y_ * NX + x_], got.at[1, x_, y], p_send.at[1], p_recv.at[1, x_], device(x, y_, z, core))
            else:
                got[1, x_, y] = part[1, y * NX + x_]

    def second(f, d):
        at = (y + d) % NY if f == 0 else (x + d) % NX
        wait(got.at[f, at, pl.ds(0, 3)], p_recv.at[f, at])
        total_ = jnp.sum(got[f, at], axis=0)
        if d:
            half[f, at] = total_
            to = device(x, at, z, core) if f == 0 else device(at, y, z, core)
            send(half.at[f, at], last.at[f, y if f == 0 else x], h_send.at[f], h_recv.at[f], to)
        else:
            last[f, at] = total_

    for f, d in ((0, 2), (0, 1), (1, 2), (0, 3), (1, 1), (1, 3), (0, 0), (1, 0)):
        second(f, d)

    g = (first_g + jnp.log2(v)) * POT
    for i in range(NL):
        gout[i] = g[:, i * NH * TS:(i + 1) * NH * TS]
    for j in range(1, NY):
        send(gout.at[zl], tpb.at[y], o_send.at[1], o_recv.at[1], device(x, (y + j) % NY, z, core))
    tpb[y] = gout[zl]
    wait(qpb.at[pl.ds(0, NL - 1)], o_recv.at[0])
    wait(tpb.at[pl.ds(0, NY - 1)], o_recv.at[1])
    qp_ref[...] = qpb[...]
    tp_ref[...] = dense(jnp.concatenate([tpb[i] for i in range(NY)], axis=1))

    totals = jnp.sum(wait_rows(3), axis=0)
    spread_rows(totals)
    total = cols[pl.ds(pl.multiple_of(mine * QS, QS), QS), :]
    for f in (0, 1):
        wait(last.at[f, pl.ds(0, 3)], h_recv.at[f])
    full = jnp.concatenate([jnp.sum(last[f], axis=0) for f in (0, 1)], axis=1)
    map_ref[...] = (full / jnp.concatenate([total] * (D // 128), axis=1)).astype(BF16)

    wait(qblk.at[pl.ds(0, CHIPS - 1)], q_send)
    wait(qblk.at[pl.ds(0, CHIPS)], q_fwd)
    for way in (0, 1):
        for p in range(PIECES):
            wait(tblk.at[pl.ds(0, reach(way, p)), pl.ds(p * PIECE, PIECE)], t_send.at[way])
    wait(tblk, s_send)
    wait(wsib, ws_send)
    wait(qmb.at[pl.ds(0, NY - 1)], m_send.at[0])
    wait(tmb.at[pl.ds(0, NL - 1)], m_send.at[1])
    wait(qpb.at[pl.ds(0, NL - 1)], o_send.at[0])
    wait(tpb.at[pl.ds(0, NY - 1)], o_send.at[1])
    for n in range(4):
        wait(rbuf.at[n, pl.ds(0, 2 * CHIPS - 1)], r_send.at[n])
    for n in range(3):
        wait(cbuf.at[n, pl.ds(0, NZ - 1)], c_send.at[n])
    for f in (0, 1):
        wait(part.at[f, pl.ds(0, 3 * NX)], p_send.at[f])
        wait(last.at[f, pl.ds(0, 3)], h_send.at[f])


def local(queries, tools, query_mass, tool_mass):
    vmem = pl.BlockSpec(memory_space=pltpu.VMEM)
    dma, V = pltpu.SemaphoreType.DMA, pltpu.VMEM
    mapped, qp, tp = pl.pallas_call(
        kernel,
        out_shape=(
            jax.ShapeDtypeStruct((QS, D), BF16),
            jax.ShapeDtypeStruct((NL, 2, 128), F32),
            jax.ShapeDtypeStruct((TB // 128, 128), F32),
        ),
        in_specs=[pl.BlockSpec(memory_space=pltpu.HBM)] * 4,
        out_specs=(vmem,) * 3,
        scratch_shapes=[
            V((2 * CHIPS, QS, D), BF16), V((NZ, TS, D), BF16), V((NZ, TS, D), BF16), V((QB, TB), F32),
            V((CHIPS, 2, QS, TB), BF16), V((CHIPS, QS, TB), BF16),
            V((2, CHIPS, QS, D // 2), F32), V((2, 4, 4, QS, D // 2), F32),
            V((2, 4, QS, D // 2), F32), V((2, 4, QS, D // 2), F32),
            V((QB, 128), F32),
            V((NL, 2, 128), F32), V((TB // 128, 128), F32),
            V((4, 8, 128), F32), V((4, 2 * CHIPS, 8, 128), F32), V((3, TB // 128, 128), F32), V((3, NZ, TB // 128, 128), F32),
            V((NY, 2, 128), F32), V((NY, 1, NH * TS), F32), V((NL, 1, NH * TS), F32),
            V((NY, 2, 128), F32), V((NL, 2, 128), F32), V((NL, 1, NH * TS), F32), V((NY, 1, NH * TS), F32),
            dma((4,)), dma, dma((CHIPS,)), dma, dma, dma((2,)), dma((2, NZ // 2, 3)), dma, dma, dma, dma((NY,)),
            dma((2,)), dma((2,)), dma((4,)), dma((4,)), dma((3,)), dma((3,)), dma((2,)), dma((2,)),
            dma((2,)), dma((2, 4)), dma((2,)), dma((2,)),
        ],
        compiler_params=pltpu.CompilerParams(
            collective_id=0, has_side_effects=True, vmem_limit_bytes=60 * 1024 * 1024
        ),
    )(queries, tools, query_mass.reshape(NL, 2, 128), tool_mass.reshape(TB // 128, 128))
    return mapped, qp.reshape(QB), tp.reshape(TB)


def solution(mesh):
    in_specs = (P(("row", "col"), None), P(("col", "row"), None), P("row"), P("col"))
    out_specs = (P(("row", "col"), None), P("row"), P("col"))
    return jax.shard_map(local, mesh=mesh, in_specs=in_specs, out_specs=out_specs, check_vma=False)
```

```python
import functools
import math

import jax
import jax.numpy as jnp
from jax import lax
from jax.experimental import pallas as pl
from jax.experimental.pallas import tpu as pltpu
from jax.sharding import PartitionSpec as P

MESH = pl.DeviceIdType.MESH
EPSILON = 0.5
F32 = jnp.float32
BF16 = jnp.bfloat16
NX, NY, NL, NH = 4, 4, 4, 4
NZ = NL * NH
CHIPS = NX * NY
D = 768
QS, TS = 32, 48
QB, TB = 2 * CHIPS * QS, NZ * TS
LOG2E = 1.4426950408889634
POT = EPSILON / LOG2E


def kernel(
    q_hbm, t_hbm, qm_hbm, tm_hbm,
    map_ref, qp_ref, tp_ref,
    qblk, tblk, tsib, plan, w, wsib, part, got, half, last, cols,
    qm_ref, tm_ref, rsend, rbuf, csend, cbuf, qmb, tms, tmb, fout, qpb, gout, tpb,
    l_sem, q_send, q_recv, q_fwd, q_sib, t_send, t_recv, s_send, s_recv, ws_send, ws_recv,
    m_send, m_recv, r_send, r_recv, c_send, c_recv, o_send, o_recv, p_send, p_recv, h_send, h_recv,
):
    row, col = lax.axis_index("row"), lax.axis_index("col")
    y, zh = row // NH, row % NH
    zl, x, core = col // (2 * NX), (col // 2) % NX, col % 2
    z = zh * NL + zl
    sib = 1 - core
    chip = y * NX + x
    mine = chip * 2 + core
    slot = zl * NH + zh

    def device(x_, y_, z_, core_):
        return (y_ * NH + z_ // NL, ((z_ % NL) * NX + x_) * 2 + core_)

    rows_at = [((y + b) % NY) * NH + zh for b in range(NY)]
    cols_at = [(zl * NX + (x + a) % NX) * 2 for a in range(NX)]
    plane = [
        (rows_at[b], cols_at[a] + core_)
        for b in (2, 1, 3, 0) for a in (2, 1, 3, 0) for core_ in (sib, core)
    ][:-1]
    others_z = [(z + d) % NZ for d in (8, 7, 9, 6, 10, 5, 11, 4, 12, 3, 13, 2, 14, 1, 15)]
    column = [device(x, y, z_, core) for z_ in others_z]

    def send(src, dst, s_sem, r_sem, dev):
        pltpu.make_async_remote_copy(
            src_ref=src, dst_ref=dst, send_sem=s_sem, recv_sem=r_sem, device_id=dev, device_id_type=MESH
        ).start()

    def wait(ref, sem):
        pltpu.make_async_copy(ref, ref, sem).wait()

    barrier = pltpu.get_barrier_semaphore()
    for near in (2, NZ - 2, 1, NZ - 1):
        peer = device(x, y, (z + near) % NZ, core)
        pl.semaphore_signal(barrier, inc=1, device_id=peer, device_id_type=MESH)

    hops = {0: 0, 1: 1, 2: 2, 3: 1}
    shifts = [(a, b) for a in (2, 1, 3, 0) for b in (2, 1, 3, 0) if (a, b) != (0, 0)]
    near_chips = [s for s in shifts if hops[s[0]] + hops[s[1]] <= 2]
    far_chips = [s for s in shifts if s not in near_chips]
    for a, b in near_chips + [(0, 0)]:
        for core_ in (sib, core) if (a, b) != (0, 0) else (sib,):
            peer = device((x + a) % NX, (y + b) % NY, z, core_)
            pl.semaphore_signal(barrier, inc=1, device_id=peer, device_id_type=MESH)

    loads = [
        pltpu.make_async_copy(t_hbm, tblk.at[slot], l_sem.at[0]),
        pltpu.make_async_copy(q_hbm, qblk.at[mine], l_sem.at[1]),
        pltpu.make_async_copy(qm_hbm, qm_ref, l_sem.at[2]),
        pltpu.make_async_copy(tm_hbm, tm_ref, l_sem.at[3]),
    ]
    for load in loads:
        load.start()
    for load in loads:
        load.wait()
    tms_all = jnp.concatenate([tm_ref[c:c + 1, :] for c in range(TB // 128)], axis=1)
    for i in range(NY):
        tms[i] = tms_all[:, i * NH * TS:(i + 1) * NH * TS]
    pl.semaphore_wait(barrier, 2 * len(near_chips) + 1 + 4)

    lane = lax.broadcasted_iota(jnp.int32, (8, 128), 1)
    zero = jnp.zeros((8, 128), F32)
    RB = 64
    NB = QB // RB

    def pick(out, block, values):
        n = values.shape[0] // 8
        for g in range(n):
            out = jnp.where(lane == block * n + g, values[g * 8:(g + 1) * 8, :], out)
        return out

    scale = LOG2E / (EPSILON * math.sqrt(D))
    HB, MB = TB // 2, 256

    def products(half):
        lanes = pl.ds(pl.multiple_of(half * HB, 128), HB)
        tools = tblk[pl.ds(half * (NZ // 2), NZ // 2)].reshape(HB, D)

        def body(i, carry):
            tops, sums = carry
            a = qblk[pl.ds(i * (MB // QS), MB // QS)].reshape(MB, D)
            s = scale * lax.dot_general(a, tools, (((1,), (1,)), ((), ())), preferred_element_type=F32)
            plan[pl.ds(pl.multiple_of(i * MB, MB), MB), lanes] = s
            top = jnp.max(s, axis=1, keepdims=True)
            total = jnp.sum(jnp.exp2(s - top), axis=1, keepdims=True)
            return pick(tops, i, top), pick(sums, i, total)

        return lax.fori_loop(0, QB // MB, body, (zero, zero))

    def t_slot(z_):
        return (z_ % NL) * NH + z_ // NL

    PIECES, PIECE = 3, TS // 3

    def t_piece(source, p):
        return tblk.at[t_slot(source), pl.ds(p * PIECE, PIECE)]

    def reach(way, p):
        return NZ // 2 if (way == 0) == (p < 2) else NZ // 2 - 1

    def t_source(way, dist):
        return (z + NZ - dist) % NZ if way == 0 else (z + dist) % NZ

    ONWARD = {0: (2, 1), 2: (4, 3), 4: (6, 5), 6: (7,), 7: (8,)}

    def t_forward(way, dist, p):
        piece = t_piece(t_source(way, dist), p)
        for there in ONWARD.get(dist, ()):
            if there <= reach(way, p):
                to = device(x, y, t_source(way, NZ + dist - there), core)
                send(piece, piece, t_send.at[way], t_recv.at[way, there - 1, p], to)

    for p in range(PIECES):
        for way in (0, 1):
            t_forward(way, 0, p)

    def q_give(a, b):
        to = device((x + a) % NX, (y + b) % NY, z, core)
        send(qblk.at[mine], qblk.at[mine], q_send, q_recv.at[chip], to)

    def q_take(a, b):
        chip_ = ((y + b) % NY) * NX + (x + a) % NX
        s = chip_ * 2 + core
        wait(qblk.at[s], q_recv.at[chip_])
        send(qblk.at[s], qblk.at[s], q_fwd, q_sib, device(x, y, z, sib))

    for a, b in near_chips:
        q_give(a, b)
    corners = [(1, 1), (3, 1), (1, 3)]
    others = [s for s in near_chips if s not in corners] + far_chips
    send(qblk.at[mine], qblk.at[mine], q_fwd, q_sib, device(x, y, z, sib))
    for j in range(1, NY):
        send(qm_ref.at[zl], qmb.at[y], m_send.at[0], m_recv.at[0], device(x, (y + j) % NY, z, core))
    qmb[y] = qm_ref[zl]
    tmb[zl] = tms[y]

    for step, dist in enumerate((2, 1, 4, 3, 6, 5, 7, 8)):
        for p in range(PIECES):
            for way in (0, 1):
                if dist <= reach(way, p):
                    wait(t_piece(t_source(way, dist), p), t_recv.at[way, dist - 1, p])
                    t_forward(way, dist, p)
        if step == 1:
            for a, b in corners:
                q_take(a, b)
            for a, b in far_chips:
                q_give(a, b)
        if 3 <= step < 7:
            for a, b in others[3 * (step - 3):3 * (step - 2)]:
                q_take(a, b)
        if step == NL - 1:
            for j in range(1, NL):
                send(tms.at[y], tmb.at[zl], m_send.at[1], m_recv.at[1], device(x, y, zh * NL + (zl + j) % NL, core))
        if step == NZ // 2 - 2:
            wait(qblk.at[pl.ds(0, CHIPS)], q_sib)
            early = products(1 - zl // 2)

    def dense(v):
        return jnp.concatenate([v[:, c * 128:(c + 1) * 128] for c in range(TB // 128)], axis=0)

    def undense(v):
        return jnp.concatenate([v[c:c + 1, :] for c in range(TB // 128)], axis=1)

    def gather_rows(n, value):
        rsend[n] = value
        rbuf[n, mine] = value

        for peer in plane:
            send(rsend.at[n], rbuf.at[n, mine], r_send.at[n], r_recv.at[n], peer)

    def wait_rows(n):
        wait(rbuf.at[n, pl.ds(0, 2 * CHIPS - 1)], r_recv.at[n])
        return rbuf[n]

    def gather_cols(n, value):
        csend[n] = value
        cbuf[n, z] = value

        for peer in column:
            send(csend.at[n], cbuf.at[n, z], c_send.at[n], c_recv.at[n], peer)

    def wait_cols(n):
        wait(cbuf.at[n, pl.ds(0, NZ - 1)], c_recv.at[n])
        return cbuf[n]

    def lse(parts):
        top = jnp.max(parts, axis=0)
        return top + jnp.log2(jnp.sum(jnp.exp2(parts - top[None]), axis=0))

    def spread_rows(value):
        for k in range(QB // 8):
            cols[k * 8:k * 8 + 8, :] = jnp.broadcast_to(value[:, k:k + 1], (8, 128))

    def wide(r0, rows):
        return jnp.concatenate([cols[pl.ds(r0, rows), :]] * (TB // 128), axis=1)

    (top_a, sum_a), (top_b, sum_b) = early, products(zl // 2)
    tops = jnp.maximum(top_a, top_b)
    sums = sum_a * jnp.exp2(top_a - tops) + sum_b * jnp.exp2(top_b - tops)
    gather_rows(0, tops + jnp.log2(sums))
    send(tblk, tsib, s_send, s_recv, device(x, y, z, sib))

    wait(qmb.at[pl.ds(0, NY - 1)], m_recv.at[0])
    wait(tmb.at[pl.ds(0, NL - 1)], m_recv.at[1])
    mass_q = jnp.zeros((8, 128), F32)
    for b in range(8):
        line = qmb[b // 2, pl.ds(b % 2, 1), :]
        spread = jnp.broadcast_to(line, (128, 128)).T
        for k in range(16):
            mass_q = jnp.where(lane == b * 16 + k, spread[k * 8:k * 8 + 8, :], mass_q)
    mass_t = jnp.concatenate([tmb[i] for i in range(NL)], axis=1)

    first_f = jnp.log2(mass_q) - lse(wait_rows(0))

    spread_rows(first_f)

    def col_max(i, top):
        r0 = pl.multiple_of(i * RB, RB)
        s = plan[pl.ds(r0, RB), :] + wide(r0, RB)
        plan[pl.ds(r0, RB), :] = s
        return jnp.maximum(top, jnp.max(s.reshape(RB // 8, 8, TB), axis=0))

    top8 = lax.fori_loop(0, NB, col_max, jnp.full((8, TB), -jnp.inf, F32))
    top = jnp.max(top8, axis=0, keepdims=True)

    def col_sum(i, acc):
        s = plan[pl.ds(pl.multiple_of(i * RB, RB), RB), :]
        return acc + jnp.sum(jnp.exp2(s - top).reshape(RB // 8, 8, TB), axis=0)

    acc = lax.fori_loop(0, NB, col_sum, jnp.zeros((8, TB), F32))
    gather_cols(0, dense(top + jnp.log2(jnp.sum(acc, axis=0, keepdims=True))))
    first_g = jnp.log2(mass_t) - undense(lse(wait_cols(0)))

    def second_rows(i, sums):
        r0 = pl.multiple_of(i * RB, RB)
        e = jnp.exp2(plan[pl.ds(r0, RB), :] + first_g)
        plan[pl.ds(r0, RB), :] = e
        return pick(sums, i, jnp.sum(e, axis=1, keepdims=True))

    def later_rows(v):
        def body(i, sums):
            e = plan[pl.ds(pl.multiple_of(i * RB, RB), RB), :] * v
            return pick(sums, i, jnp.sum(e, axis=1, keepdims=True))
        return lax.fori_loop(0, NB, body, zero)

    def later_cols():
        def body(i, acc):
            r0 = pl.multiple_of(i * RB, RB)
            e = plan[pl.ds(r0, RB), :] * wide(r0, RB)
            return acc + jnp.sum(e.reshape(RB // 8, 8, TB), axis=0)
        acc = lax.fori_loop(0, NB, body, jnp.zeros((8, TB), F32))
        return dense(jnp.sum(acc, axis=0, keepdims=True))

    gather_rows(1, lax.fori_loop(0, NB, second_rows, zero))
    u = mass_q / jnp.sum(wait_rows(1), axis=0)
    spread_rows(u)
    gather_cols(1, later_cols())
    v = mass_t / undense(jnp.sum(wait_cols(1), axis=0))
    gather_rows(2, later_rows(v))
    u = mass_q / jnp.sum(wait_rows(2), axis=0)
    spread_rows(u)
    gather_cols(2, later_cols())

    f = (first_f + jnp.log2(u)) * POT
    for b in range(8):
        block = jnp.concatenate(
            [jnp.broadcast_to(f[:, b * 16 + k:b * 16 + k + 1], (8, 128)) for k in range(16)], axis=0
        )
        fout[b // 2, pl.ds(b % 2, 1), :] = block.T[0:1, :]
    for j in range(1, NL):
        send(fout.at[y], qpb.at[zl], o_send.at[0], o_recv.at[0], device(x, y, zh * NL + (zl + j) % NL, core))
    qpb[zl] = fout[y]
    v = mass_t / undense(jnp.sum(wait_cols(2), axis=0))

    PB = 2 * QS

    def weights(y_, i, sums):
        c = y_ * NX + i
        r0 = pl.multiple_of(c * PB, PB)
        e = (plan[pl.ds(r0, PB), :] * wide(r0, PB) * v).astype(BF16)
        w[c] = e.reshape(2, QS, TB)
        return pick(sums, c, jnp.sum(e.astype(F32), axis=1, keepdims=True))

    wait(tsib, s_recv)
    sums = zero
    for h in range(NY):
        y_ = (y + (2, 1, 3, 0)[h]) % NY
        sums = lax.fori_loop(0, NX, functools.partial(weights, y_), sums)
        send(w.at[pl.ds(y_ * NX, NX), sib], wsib.at[pl.ds(y_ * NX, NX)], ws_send, ws_recv.at[h], device(x, y, z, sib))

    own, other = tblk[...].reshape(TB, D), tsib[...].reshape(TB, D)
    HD = D // 2
    for h, dy in enumerate((2, 1, 3, 0)):
        y_ = (y + dy) % NY
        a = w[pl.ds(y_ * NX, NX), core].reshape(NX * QS, TB)
        p = jnp.dot(a, own, preferred_element_type=F32)
        wait(wsib.at[pl.ds(y_ * NX, NX)], ws_recv.at[h])
        b = wsib[pl.ds(y_ * NX, NX)].reshape(NX * QS, TB)
        p = p + jnp.dot(b, other, preferred_element_type=F32)
        for f in (0, 1):
            part[f, pl.ds(y_ * NX, NX)] = p[:, f * HD:(f + 1) * HD].reshape(NX, QS, HD)
        for dx in (2, 1, 3, 0):
            x_ = (x + dx) % NX
            if dx:
                send(part.at[0, y_ * NX + x_], got.at[0, y_, x], p_send.at[0], p_recv.at[0, y_], device(x_, y, z, core))
            else:
                got[0, y_, x] = part[0, y_ * NX + x]
            if dy:
                send(part.at[1, y_ * NX + x_], got.at[1, x_, y], p_send.at[1], p_recv.at[1, x_], device(x, y_, z, core))
            else:
                got[1, x_, y] = part[1, y * NX + x_]

    gather_rows(3, sums)

    def second(f, d):
        at = (y + d) % NY if f == 0 else (x + d) % NX
        wait(got.at[f, at, pl.ds(0, 3)], p_recv.at[f, at])
        total_ = jnp.sum(got[f, at], axis=0)
        if d:
            half[f, at] = total_
            to = device(x, at, z, core) if f == 0 else device(at, y, z, core)
            send(half.at[f, at], last.at[f, y if f == 0 else x], h_send.at[f], h_recv.at[f], to)
        else:
            last[f, at] = total_

    for f, d in ((0, 2), (0, 1), (1, 2), (0, 3), (1, 1), (1, 3), (0, 0), (1, 0)):
        second(f, d)

    g = (first_g + jnp.log2(v)) * POT
    for i in range(NL):
        gout[i] = g[:, i * NH * TS:(i + 1) * NH * TS]
    for j in range(1, NY):
        send(gout.at[zl], tpb.at[y], o_send.at[1], o_recv.at[1], device(x, (y + j) % NY, z, core))
    tpb[y] = gout[zl]
    wait(qpb.at[pl.ds(0, NL - 1)], o_recv.at[0])
    wait(tpb.at[pl.ds(0, NY - 1)], o_recv.at[1])
    qp_ref[...] = qpb[...]
    tp_ref[...] = dense(jnp.concatenate([tpb[i] for i in range(NY)], axis=1))

    totals = jnp.sum(wait_rows(3), axis=0)
    spread_rows(totals)
    total = cols[pl.ds(pl.multiple_of(mine * QS, QS), QS), :]
    for f in (0, 1):
        wait(last.at[f, pl.ds(0, 3)], h_recv.at[f])
    full = jnp.concatenate([jnp.sum(last[f], axis=0) for f in (0, 1)], axis=1)
    map_ref[...] = (full / jnp.concatenate([total] * (D // 128), axis=1)).astype(BF16)

    wait(qblk.at[pl.ds(0, CHIPS - 1)], q_send)
    wait(qblk.at[pl.ds(0, CHIPS)], q_fwd)
    for way in (0, 1):
        for p in range(PIECES):
            wait(tblk.at[pl.ds(0, reach(way, p)), pl.ds(p * PIECE, PIECE)], t_send.at[way])
    wait(tblk, s_send)
    wait(wsib, ws_send)
    wait(qmb.at[pl.ds(0, NY - 1)], m_send.at[0])
    wait(tmb.at[pl.ds(0, NL - 1)], m_send.at[1])
    wait(qpb.at[pl.ds(0, NL - 1)], o_send.at[0])
    wait(tpb.at[pl.ds(0, NY - 1)], o_send.at[1])
    for n in range(4):
        wait(rbuf.at[n, pl.ds(0, 2 * CHIPS - 1)], r_send.at[n])
    for n in range(3):
        wait(cbuf.at[n, pl.ds(0, NZ - 1)], c_send.at[n])
    for f in (0, 1):
        wait(part.at[f, pl.ds(0, 3 * NX)], p_send.at[f])
        wait(last.at[f, pl.ds(0, 3)], h_send.at[f])


def local(queries, tools, query_mass, tool_mass):
    vmem = pl.BlockSpec(memory_space=pltpu.VMEM)
    dma, V = pltpu.SemaphoreType.DMA, pltpu.VMEM
    mapped, qp, tp = pl.pallas_call(
        kernel,
        out_shape=(
            jax.ShapeDtypeStruct((QS, D), BF16),
            jax.ShapeDtypeStruct((NL, 2, 128), F32),
            jax.ShapeDtypeStruct((TB // 128, 128), F32),
        ),
        in_specs=[pl.BlockSpec(memory_space=pltpu.HBM)] * 4,
        out_specs=(vmem,) * 3,
        scratch_shapes=[
            V((2 * CHIPS, QS, D), BF16), V((NZ, TS, D), BF16), V((NZ, TS, D), BF16), V((QB, TB), F32),
            V((CHIPS, 2, QS, TB), BF16), V((CHIPS, QS, TB), BF16),
            V((2, CHIPS, QS, D // 2), F32), V((2, 4, 4, QS, D // 2), F32),
            V((2, 4, QS, D // 2), F32), V((2, 4, QS, D // 2), F32),
            V((QB, 128), F32),
            V((NL, 2, 128), F32), V((TB // 128, 128), F32),
            V((4, 8, 128), F32), V((4, 2 * CHIPS, 8, 128), F32), V((3, TB // 128, 128), F32), V((3, NZ, TB // 128, 128), F32),
            V((NY, 2, 128), F32), V((NY, 1, NH * TS), F32), V((NL, 1, NH * TS), F32),
            V((NY, 2, 128), F32), V((NL, 2, 128), F32), V((NL, 1, NH * TS), F32), V((NY, 1, NH * TS), F32),
            dma((4,)), dma, dma((CHIPS,)), dma, dma, dma((2,)), dma((2, NZ // 2, 3)), dma, dma, dma, dma((NY,)),
            dma((2,)), dma((2,)), dma((4,)), dma((4,)), dma((3,)), dma((3,)), dma((2,)), dma((2,)),
            dma((2,)), dma((2, 4)), dma((2,)), dma((2,)),
        ],
        compiler_params=pltpu.CompilerParams(
            collective_id=0, has_side_effects=True, vmem_limit_bytes=60 * 1024 * 1024
        ),
    )(queries, tools, query_mass.reshape(NL, 2, 128), tool_mass.reshape(TB // 128, 128))
    return mapped, qp.reshape(QB), tp.reshape(TB)


def solution(mesh):
    in_specs = (P(("row", "col"), None), P(("col", "row"), None), P("row"), P("col"))
    out_specs = (P(("row", "col"), None), P("row"), P("col"))
    return jax.shard_map(local, mesh=mesh, in_specs=in_specs, out_specs=out_specs, check_vma=False)
```

```python
import functools
import math

import jax
import jax.numpy as jnp
from jax import lax
from jax.experimental import pallas as pl
from jax.experimental.pallas import tpu as pltpu
from jax.sharding import PartitionSpec as P

MESH = pl.DeviceIdType.MESH
EPSILON = 0.5
F32 = jnp.float32
BF16 = jnp.bfloat16
NX, NY, NL, NH = 4, 4, 4, 4
NZ = NL * NH
CHIPS = NX * NY
D = 768
QS, TS = 32, 48
QB, TB = 2 * CHIPS * QS, NZ * TS
LOG2E = 1.4426950408889634
POT = EPSILON / LOG2E


def kernel(
    q_hbm, t_hbm, qm_hbm, tm_hbm,
    map_ref, qp_ref, tp_ref,
    qblk, tblk, tsib, plan, w, wsib, part, got, half, last, cols,
    qm_ref, tm_ref, rsend, rbuf, csend, cbuf, qmb, tms, tmb, fout, qpb, gout, tpb,
    l_sem, q_send, q_recv, q_fwd, q_sib, t_send, t_recv, s_send, s_recv, ws_send, ws_recv,
    m_send, m_recv, r_send, r_recv, c_send, c_recv, o_send, o_recv, p_send, p_recv, h_send, h_recv,
):
    row, col = lax.axis_index("row"), lax.axis_index("col")
    y, zh = row // NH, row % NH
    zl, x, core = col // (2 * NX), (col // 2) % NX, col % 2
    z = zh * NL + zl
    sib = 1 - core
    chip = y * NX + x
    mine = chip * 2 + core
    slot = zl * NH + zh

    def device(x_, y_, z_, core_):
        return (y_ * NH + z_ // NL, ((z_ % NL) * NX + x_) * 2 + core_)

    rows_at = [((y + b) % NY) * NH + zh for b in range(NY)]
    cols_at = [(zl * NX + (x + a) % NX) * 2 for a in range(NX)]
    plane = [
        (rows_at[b], cols_at[a] + core_)
        for b in (2, 1, 3, 0) for a in (2, 1, 3, 0) for core_ in (sib, core)
    ][:-1]
    others_z = [(z + d) % NZ for d in (8, 7, 9, 6, 10, 5, 11, 4, 12, 3, 13, 2, 14, 1, 15)]
    column = [device(x, y, z_, core) for z_ in others_z]

    def send(src, dst, s_sem, r_sem, dev):
        pltpu.make_async_remote_copy(
            src_ref=src, dst_ref=dst, send_sem=s_sem, recv_sem=r_sem, device_id=dev, device_id_type=MESH
        ).start()

    def wait(ref, sem):
        pltpu.make_async_copy(ref, ref, sem).wait()

    barrier = pltpu.get_barrier_semaphore()
    for near in (2, NZ - 2, 1, NZ - 1):
        peer = device(x, y, (z + near) % NZ, core)
        pl.semaphore_signal(barrier, inc=1, device_id=peer, device_id_type=MESH)

    hops = {0: 0, 1: 1, 2: 2, 3: 1}
    shifts = [(a, b) for a in (2, 1, 3, 0) for b in (2, 1, 3, 0) if (a, b) != (0, 0)]
    near_chips = [s for s in shifts if hops[s[0]] + hops[s[1]] <= 2]
    far_chips = [s for s in shifts if s not in near_chips]
    for a, b in near_chips + [(0, 0)]:
        for core_ in (sib, core) if (a, b) != (0, 0) else (sib,):
            peer = device((x + a) % NX, (y + b) % NY, z, core_)
            pl.semaphore_signal(barrier, inc=1, device_id=peer, device_id_type=MESH)

    loads = [
        pltpu.make_async_copy(t_hbm, tblk.at[slot], l_sem.at[0]),
        pltpu.make_async_copy(q_hbm, qblk.at[mine], l_sem.at[1]),
        pltpu.make_async_copy(qm_hbm, qm_ref, l_sem.at[2]),
        pltpu.make_async_copy(tm_hbm, tm_ref, l_sem.at[3]),
    ]
    for load in loads:
        load.start()
    for load in loads:
        load.wait()
    tms_all = jnp.concatenate([tm_ref[c:c + 1, :] for c in range(TB // 128)], axis=1)
    for i in range(NY):
        tms[i] = tms_all[:, i * NH * TS:(i + 1) * NH * TS]
    pl.semaphore_wait(barrier, 2 * len(near_chips) + 1 + 4)

    lane = lax.broadcasted_iota(jnp.int32, (8, 128), 1)
    zero = jnp.zeros((8, 128), F32)
    RB = 64
    NB = QB // RB

    def pick(out, block, values):
        n = values.shape[0] // 8
        for g in range(n):
            out = jnp.where(lane == block * n + g, values[g * 8:(g + 1) * 8, :], out)
        return out

    scale = LOG2E / (EPSILON * math.sqrt(D))
    HB, MB = TB // 2, 256

    def products(half):
        lanes = pl.ds(pl.multiple_of(half * HB, 128), HB)
        tools = tblk[pl.ds(half * (NZ // 2), NZ // 2)].reshape(HB, D)

        def body(i, carry):
            tops, sums = carry
            a = qblk[pl.ds(i * (MB // QS), MB // QS)].reshape(MB, D)
            s = scale * lax.dot_general(a, tools, (((1,), (1,)), ((), ())), preferred_element_type=F32)
            plan[pl.ds(pl.multiple_of(i * MB, MB), MB), lanes] = s
            top = jnp.max(s, axis=1, keepdims=True)
            total = jnp.sum(jnp.exp2(s - top), axis=1, keepdims=True)
            return pick(tops, i, top), pick(sums, i, total)

        return lax.fori_loop(0, QB // MB, body, (zero, zero), unroll=4)

    def t_slot(z_):
        return (z_ % NL) * NH + z_ // NL

    PIECES, PIECE = 3, TS // 3

    def t_piece(source, p):
        return tblk.at[t_slot(source), pl.ds(p * PIECE, PIECE)]

    def reach(way, p):
        return NZ // 2 if (way == 0) == (p < 2) else NZ // 2 - 1

    def t_source(way, dist):
        return (z + NZ - dist) % NZ if way == 0 else (z + dist) % NZ

    ONWARD = {0: (2, 1), 2: (4, 3), 4: (6, 5), 6: (7,), 7: (8,)}

    def t_forward(way, dist, p):
        piece = t_piece(t_source(way, dist), p)
        for there in ONWARD.get(dist, ()):
            if there <= reach(way, p):
                to = device(x, y, t_source(way, NZ + dist - there), core)
                send(piece, piece, t_send.at[way], t_recv.at[way, there - 1, p], to)

    for p in range(PIECES):
        for way in (0, 1):
            t_forward(way, 0, p)

    def q_give(a, b):
        to = device((x + a) % NX, (y + b) % NY, z, core)
        send(qblk.at[mine], qblk.at[mine], q_send, q_recv.at[chip], to)

    def q_take(a, b):
        chip_ = ((y + b) % NY) * NX + (x + a) % NX
        s = chip_ * 2 + core
        wait(qblk.at[s], q_recv.at[chip_])
        send(qblk.at[s], qblk.at[s], q_fwd, q_sib, device(x, y, z, sib))

    for a, b in near_chips:
        q_give(a, b)
    corners = [(1, 1), (3, 1), (1, 3)]
    others = [s for s in near_chips if s not in corners] + far_chips
    send(qblk.at[mine], qblk.at[mine], q_fwd, q_sib, device(x, y, z, sib))
    for j in range(1, NY):
        send(qm_ref.at[zl], qmb.at[y], m_send.at[0], m_recv.at[0], device(x, (y + j) % NY, z, core))
    qmb[y] = qm_ref[zl]
    tmb[zl] = tms[y]

    for step, dist in enumerate((2, 1, 4, 3, 6, 5, 7, 8)):
        for p in range(PIECES):
            for way in (0, 1):
                if dist <= reach(way, p):
                    wait(t_piece(t_source(way, dist), p), t_recv.at[way, dist - 1, p])
                    t_forward(way, dist, p)
        if step == 1:
            for a, b in corners:
                q_take(a, b)
            for a, b in far_chips:
                q_give(a, b)
        if 3 <= step < 7:
            for a, b in others[3 * (step - 3):3 * (step - 2)]:
                q_take(a, b)
        if step == NL - 1:
            for j in range(1, NL):
                send(tms.at[y], tmb.at[zl], m_send.at[1], m_recv.at[1], device(x, y, zh * NL + (zl + j) % NL, core))
        if step == NZ // 2 - 2:
            wait(qblk.at[pl.ds(0, CHIPS)], q_sib)
            early = products(1 - zl // 2)

    def dense(v):
        return jnp.concatenate([v[:, c * 128:(c + 1) * 128] for c in range(TB // 128)], axis=0)

    def undense(v):
        return jnp.concatenate([v[c:c + 1, :] for c in range(TB // 128)], axis=1)

    def gather_rows(n, value):
        rsend[n] = value
        rbuf[n, mine] = value

        for peer in plane:
            send(rsend.at[n], rbuf.at[n, mine], r_send.at[n], r_recv.at[n], peer)

    def wait_rows(n):
        wait(rbuf.at[n, pl.ds(0, 2 * CHIPS - 1)], r_recv.at[n])
        return rbuf[n]

    def gather_cols(n, value):
        csend[n] = value
        cbuf[n, z] = value

        for peer in column:
            send(csend.at[n], cbuf.at[n, z], c_send.at[n], c_recv.at[n], peer)

    def wait_cols(n):
        wait(cbuf.at[n, pl.ds(0, NZ - 1)], c_recv.at[n])
        return cbuf[n]

    def lse(parts):
        top = jnp.max(parts, axis=0)
        return top + jnp.log2(jnp.sum(jnp.exp2(parts - top[None]), axis=0))

    def spread_rows(value):
        for k in range(QB // 8):
            cols[k * 8:k * 8 + 8, :] = jnp.broadcast_to(value[:, k:k + 1], (8, 128))

    def wide(r0, rows):
        return jnp.concatenate([cols[pl.ds(r0, rows), :]] * (TB // 128), axis=1)

    (top_a, sum_a), (top_b, sum_b) = early, products(zl // 2)
    tops = jnp.maximum(top_a, top_b)
    sums = sum_a * jnp.exp2(top_a - tops) + sum_b * jnp.exp2(top_b - tops)
    gather_rows(0, tops + jnp.log2(sums))
    send(tblk, tsib, s_send, s_recv, device(x, y, z, sib))

    wait(qmb.at[pl.ds(0, NY - 1)], m_recv.at[0])
    wait(tmb.at[pl.ds(0, NL - 1)], m_recv.at[1])
    mass_q = jnp.zeros((8, 128), F32)
    for b in range(8):
        line = qmb[b // 2, pl.ds(b % 2, 1), :]
        spread = jnp.broadcast_to(line, (128, 128)).T
        for k in range(16):
            mass_q = jnp.where(lane == b * 16 + k, spread[k * 8:k * 8 + 8, :], mass_q)
    mass_t = jnp.concatenate([tmb[i] for i in range(NL)], axis=1)

    first_f = jnp.log2(mass_q) - lse(wait_rows(0))

    spread_rows(first_f)

    def col_max(i, top):
        r0 = pl.multiple_of(i * RB, RB)
        s = plan[pl.ds(r0, RB), :] + wide(r0, RB)
        plan[pl.ds(r0, RB), :] = s
        return jnp.maximum(top, jnp.max(s.reshape(RB // 8, 8, TB), axis=0))

    top8 = lax.fori_loop(0, NB, col_max, jnp.full((8, TB), -jnp.inf, F32), unroll=4)
    top = jnp.max(top8, axis=0, keepdims=True)

    def col_sum(i, acc):
        s = plan[pl.ds(pl.multiple_of(i * RB, RB), RB), :]
        return acc + jnp.sum(jnp.exp2(s - top).reshape(RB // 8, 8, TB), axis=0)

    acc = lax.fori_loop(0, NB, col_sum, jnp.zeros((8, TB), F32), unroll=4)
    gather_cols(0, dense(top + jnp.log2(jnp.sum(acc, axis=0, keepdims=True))))
    first_g = jnp.log2(mass_t) - undense(lse(wait_cols(0)))

    def second_rows(i, sums):
        r0 = pl.multiple_of(i * RB, RB)
        e = jnp.exp2(plan[pl.ds(r0, RB), :] + first_g)
        plan[pl.ds(r0, RB), :] = e
        return pick(sums, i, jnp.sum(e, axis=1, keepdims=True))

    def later_rows(v):
        def body(i, sums):
            e = plan[pl.ds(pl.multiple_of(i * RB, RB), RB), :] * v
            return pick(sums, i, jnp.sum(e, axis=1, keepdims=True))
        return lax.fori_loop(0, NB, body, zero, unroll=4)

    def later_cols():
        def body(i, acc):
            r0 = pl.multiple_of(i * RB, RB)
            e = plan[pl.ds(r0, RB), :] * wide(r0, RB)
            return acc + jnp.sum(e.reshape(RB // 8, 8, TB), axis=0)
        acc = lax.fori_loop(0, NB, body, jnp.zeros((8, TB), F32), unroll=4)
        return dense(jnp.sum(acc, axis=0, keepdims=True))

    gather_rows(1, lax.fori_loop(0, NB, second_rows, zero, unroll=4))
    u = mass_q / jnp.sum(wait_rows(1), axis=0)
    spread_rows(u)
    gather_cols(1, later_cols())
    v = mass_t / undense(jnp.sum(wait_cols(1), axis=0))
    gather_rows(2, later_rows(v))
    u = mass_q / jnp.sum(wait_rows(2), axis=0)
    spread_rows(u)
    gather_cols(2, later_cols())

    f = (first_f + jnp.log2(u)) * POT
    for b in range(8):
        block = jnp.concatenate(
            [jnp.broadcast_to(f[:, b * 16 + k:b * 16 + k + 1], (8, 128)) for k in range(16)], axis=0
        )
        fout[b // 2, pl.ds(b % 2, 1), :] = block.T[0:1, :]
    for j in range(1, NL):
        send(fout.at[y], qpb.at[zl], o_send.at[0], o_recv.at[0], device(x, y, zh * NL + (zl + j) % NL, core))
    qpb[zl] = fout[y]
    v = mass_t / undense(jnp.sum(wait_cols(2), axis=0))

    PB = 2 * QS

    def weights(y_, i, sums):
        c = y_ * NX + i
        r0 = pl.multiple_of(c * PB, PB)
        e = (plan[pl.ds(r0, PB), :] * wide(r0, PB) * v).astype(BF16)
        w[c] = e.reshape(2, QS, TB)
        return pick(sums, c, jnp.sum(e.astype(F32), axis=1, keepdims=True))

    wait(tsib, s_recv)
    sums = zero
    for h in range(NY):
        y_ = (y + (2, 1, 3, 0)[h]) % NY
        sums = lax.fori_loop(0, NX, functools.partial(weights, y_), sums, unroll=2)
        send(w.at[pl.ds(y_ * NX, NX), sib], wsib.at[pl.ds(y_ * NX, NX)], ws_send, ws_recv.at[h], device(x, y, z, sib))

    own, other = tblk[...].reshape(TB, D), tsib[...].reshape(TB, D)
    HD = D // 2
    for h, dy in enumerate((2, 1, 3, 0)):
        y_ = (y + dy) % NY
        a = w[pl.ds(y_ * NX, NX), core].reshape(NX * QS, TB)
        p = jnp.dot(a, own, preferred_element_type=F32)
        wait(wsib.at[pl.ds(y_ * NX, NX)], ws_recv.at[h])
        b = wsib[pl.ds(y_ * NX, NX)].reshape(NX * QS, TB)
        p = p + jnp.dot(b, other, preferred_element_type=F32)
        for f in (0, 1):
            part[f, pl.ds(y_ * NX, NX)] = p[:, f * HD:(f + 1) * HD].reshape(NX, QS, HD)
        for dx in (2, 1, 3, 0):
            x_ = (x + dx) % NX
            if dx:
                send(part.at[0, y_ * NX + x_], got.at[0, y_, x], p_send.at[0], p_recv.at[0, y_], device(x_, y, z, core))
            else:
                got[0, y_, x] = part[0, y_ * NX + x]
            if dy:
                send(part.at[1, y_ * NX + x_], got.at[1, x_, y], p_send.at[1], p_recv.at[1, x_], device(x, y_, z, core))
            else:
                got[1, x_, y] = part[1, y * NX + x_]

    gather_rows(3, sums)

    def second(f, d):
        at = (y + d) % NY if f == 0 else (x + d) % NX
        wait(got.at[f, at, pl.ds(0, 3)], p_recv.at[f, at])
        total_ = jnp.sum(got[f, at], axis=0)
        if d:
            half[f, at] = total_
            to = device(x, at, z, core) if f == 0 else device(at, y, z, core)
            send(half.at[f, at], last.at[f, y if f == 0 else x], h_send.at[f], h_recv.at[f], to)
        else:
            last[f, at] = total_

    for f, d in ((0, 2), (0, 1), (1, 2), (0, 3), (1, 1), (1, 3), (0, 0), (1, 0)):
        second(f, d)

    g = (first_g + jnp.log2(v)) * POT
    for i in range(NL):
        gout[i] = g[:, i * NH * TS:(i + 1) * NH * TS]
    for j in range(1, NY):
        send(gout.at[zl], tpb.at[y], o_send.at[1], o_recv.at[1], device(x, (y + j) % NY, z, core))
    tpb[y] = gout[zl]
    wait(qpb.at[pl.ds(0, NL - 1)], o_recv.at[0])
    wait(tpb.at[pl.ds(0, NY - 1)], o_recv.at[1])
    qp_ref[...] = qpb[...]
    tp_ref[...] = dense(jnp.concatenate([tpb[i] for i in range(NY)], axis=1))

    totals = jnp.sum(wait_rows(3), axis=0)
    spread_rows(totals)
    total = cols[pl.ds(pl.multiple_of(mine * QS, QS), QS), :]
    for f in (0, 1):
        wait(last.at[f, pl.ds(0, 3)], h_recv.at[f])
    full = jnp.concatenate([jnp.sum(last[f], axis=0) for f in (0, 1)], axis=1)
    map_ref[...] = (full / jnp.concatenate([total] * (D // 128), axis=1)).astype(BF16)

    wait(qblk.at[pl.ds(0, CHIPS - 1)], q_send)
    wait(qblk.at[pl.ds(0, CHIPS)], q_fwd)
    for way in (0, 1):
        for p in range(PIECES):
            wait(tblk.at[pl.ds(0, reach(way, p)), pl.ds(p * PIECE, PIECE)], t_send.at[way])
    wait(tblk, s_send)
    wait(wsib, ws_send)
    wait(qmb.at[pl.ds(0, NY - 1)], m_send.at[0])
    wait(tmb.at[pl.ds(0, NL - 1)], m_send.at[1])
    wait(qpb.at[pl.ds(0, NL - 1)], o_send.at[0])
    wait(tpb.at[pl.ds(0, NY - 1)], o_send.at[1])
    for n in range(4):
        wait(rbuf.at[n, pl.ds(0, 2 * CHIPS - 1)], r_send.at[n])
    for n in range(3):
        wait(cbuf.at[n, pl.ds(0, NZ - 1)], c_send.at[n])
    for f in (0, 1):
        wait(part.at[f, pl.ds(0, 3 * NX)], p_send.at[f])
        wait(last.at[f, pl.ds(0, 3)], h_send.at[f])


def local(queries, tools, query_mass, tool_mass):
    vmem = pl.BlockSpec(memory_space=pltpu.VMEM)
    dma, V = pltpu.SemaphoreType.DMA, pltpu.VMEM
    mapped, qp, tp = pl.pallas_call(
        kernel,
        out_shape=(
            jax.ShapeDtypeStruct((QS, D), BF16),
            jax.ShapeDtypeStruct((NL, 2, 128), F32),
            jax.ShapeDtypeStruct((TB // 128, 128), F32),
        ),
        in_specs=[pl.BlockSpec(memory_space=pltpu.HBM)] * 4,
        out_specs=(vmem,) * 3,
        scratch_shapes=[
            V((2 * CHIPS, QS, D), BF16), V((NZ, TS, D), BF16), V((NZ, TS, D), BF16), V((QB, TB), F32),
            V((CHIPS, 2, QS, TB), BF16), V((CHIPS, QS, TB), BF16),
            V((2, CHIPS, QS, D // 2), F32), V((2, 4, 4, QS, D // 2), F32),
            V((2, 4, QS, D // 2), F32), V((2, 4, QS, D // 2), F32),
            V((QB, 128), F32),
            V((NL, 2, 128), F32), V((TB // 128, 128), F32),
            V((4, 8, 128), F32), V((4, 2 * CHIPS, 8, 128), F32), V((3, TB // 128, 128), F32), V((3, NZ, TB // 128, 128), F32),
            V((NY, 2, 128), F32), V((NY, 1, NH * TS), F32), V((NL, 1, NH * TS), F32),
            V((NY, 2, 128), F32), V((NL, 2, 128), F32), V((NL, 1, NH * TS), F32), V((NY, 1, NH * TS), F32),
            dma((4,)), dma, dma((CHIPS,)), dma, dma, dma((2,)), dma((2, NZ // 2, 3)), dma, dma, dma, dma((NY,)),
            dma((2,)), dma((2,)), dma((4,)), dma((4,)), dma((3,)), dma((3,)), dma((2,)), dma((2,)),
            dma((2,)), dma((2, 4)), dma((2,)), dma((2,)),
        ],
        compiler_params=pltpu.CompilerParams(
            collective_id=0, has_side_effects=True, vmem_limit_bytes=60 * 1024 * 1024
        ),
    )(queries, tools, query_mass.reshape(NL, 2, 128), tool_mass.reshape(TB // 128, 128))
    return mapped, qp.reshape(QB), tp.reshape(TB)


def solution(mesh):
    in_specs = (P(("row", "col"), None), P(("col", "row"), None), P("row"), P("col"))
    out_specs = (P(("row", "col"), None), P("row"), P("col"))
    return jax.shard_map(local, mesh=mesh, in_specs=in_specs, out_specs=out_specs, check_vma=False)
```

```python
import functools
import math

import jax
import jax.numpy as jnp
from jax import lax
from jax.experimental import pallas as pl
from jax.experimental.pallas import tpu as pltpu
from jax.sharding import PartitionSpec as P

MESH = pl.DeviceIdType.MESH
EPSILON = 0.5
F32 = jnp.float32
BF16 = jnp.bfloat16
NX, NY, NL, NH = 4, 4, 4, 4
NZ = NL * NH
CHIPS = NX * NY
D = 768
QS, TS = 32, 48
QB, TB = 2 * CHIPS * QS, NZ * TS
LOG2E = 1.4426950408889634
POT = EPSILON / LOG2E


def kernel(
    q_hbm, t_hbm, qm_hbm, tm_hbm,
    map_ref, qp_ref, tp_ref,
    qblk, tblk, tsib, plan, w, wsib, part, got, half, last, cols,
    qm_ref, tm_ref, rsend, rbuf, csend, cbuf, qmb, tms, tmb, fout, qpb, gout, tpb,
    l_sem, q_send, q_recv, q_fwd, q_sib, t_send, t_recv, s_send, s_recv, ws_send, ws_recv,
    m_send, m_recv, r_send, r_recv, c_send, c_recv, o_send, o_recv, p_send, p_recv, h_send, h_recv,
):
    row, col = lax.axis_index("row"), lax.axis_index("col")
    y, zh = row // NH, row % NH
    zl, x, core = col // (2 * NX), (col // 2) % NX, col % 2
    z = zh * NL + zl
    sib = 1 - core
    chip = y * NX + x
    mine = chip * 2 + core
    slot = zl * NH + zh

    def device(x_, y_, z_, core_):
        return (y_ * NH + z_ // NL, ((z_ % NL) * NX + x_) * 2 + core_)

    rows_at = [((y + b) % NY) * NH + zh for b in range(NY)]
    cols_at = [(zl * NX + (x + a) % NX) * 2 for a in range(NX)]
    plane = [
        (rows_at[b], cols_at[a] + core_)
        for b in (2, 1, 3, 0) for a in (2, 1, 3, 0) for core_ in (sib, core)
    ][:-1]
    others_z = [(z + d) % NZ for d in (8, 7, 9, 6, 10, 5, 11, 4, 12, 3, 13, 2, 14, 1, 15)]
    column = [device(x, y, z_, core) for z_ in others_z]

    def send(src, dst, s_sem, r_sem, dev):
        pltpu.make_async_remote_copy(
            src_ref=src, dst_ref=dst, send_sem=s_sem, recv_sem=r_sem, device_id=dev, device_id_type=MESH
        ).start()

    def wait(ref, sem):
        pltpu.make_async_copy(ref, ref, sem).wait()

    barrier = pltpu.get_barrier_semaphore()
    for near in (2, NZ - 2, 1, NZ - 1):
        peer = device(x, y, (z + near) % NZ, core)
        pl.semaphore_signal(barrier, inc=1, device_id=peer, device_id_type=MESH)

    hops = {0: 0, 1: 1, 2: 2, 3: 1}
    shifts = [(a, b) for a in (2, 1, 3, 0) for b in (2, 1, 3, 0) if (a, b) != (0, 0)]
    near_chips = [s for s in shifts if hops[s[0]] + hops[s[1]] <= 2]
    far_chips = [s for s in shifts if s not in near_chips]
    for a, b in near_chips + [(0, 0)]:
        for core_ in (sib, core) if (a, b) != (0, 0) else (sib,):
            peer = device((x + a) % NX, (y + b) % NY, z, core_)
            pl.semaphore_signal(barrier, inc=1, device_id=peer, device_id_type=MESH)

    loads = [
        pltpu.make_async_copy(t_hbm, tblk.at[slot], l_sem.at[0]),
        pltpu.make_async_copy(q_hbm, qblk.at[mine], l_sem.at[1]),
        pltpu.make_async_copy(qm_hbm, qm_ref, l_sem.at[2]),
        pltpu.make_async_copy(tm_hbm, tm_ref, l_sem.at[3]),
    ]
    for load in loads:
        load.start()
    for load in loads:
        load.wait()
    tms_all = jnp.concatenate([tm_ref[c:c + 1, :] for c in range(TB // 128)], axis=1)
    for i in range(NY):
        tms[i] = tms_all[:, i * NH * TS:(i + 1) * NH * TS]
    pl.semaphore_wait(barrier, 2 * len(near_chips) + 1 + 4)

    lane = lax.broadcasted_iota(jnp.int32, (8, 128), 1)
    zero = jnp.zeros((8, 128), F32)
    RB = 64
    NB = QB // RB

    def pick(out, block, values):
        n = values.shape[0] // 8
        for g in range(n):
            out = jnp.where(lane == block * n + g, values[g * 8:(g + 1) * 8, :], out)
        return out

    scale = LOG2E / (EPSILON * math.sqrt(D))
    HB, MB = TB // 2, 256

    def products(half):
        lanes = pl.ds(pl.multiple_of(half * HB, 128), HB)
        tools = tblk[pl.ds(half * (NZ // 2), NZ // 2)].reshape(HB, D)

        def body(i, carry):
            tops, sums = carry
            a = qblk[pl.ds(i * (MB // QS), MB // QS)].reshape(MB, D)
            s = scale * lax.dot_general(a, tools, (((1,), (1,)), ((), ())), preferred_element_type=F32)
            plan[pl.ds(pl.multiple_of(i * MB, MB), MB), lanes] = s
            top = jnp.max(s, axis=1, keepdims=True)
            total = jnp.sum(jnp.exp2(s - top), axis=1, keepdims=True)
            return pick(tops, i, top), pick(sums, i, total)

        return lax.fori_loop(0, QB // MB, body, (zero, zero), unroll=4)

    def t_slot(z_):
        return (z_ % NL) * NH + z_ // NL

    PIECES, PIECE = 3, TS // 3

    def t_piece(source, p):
        return tblk.at[t_slot(source), pl.ds(p * PIECE, PIECE)]

    def reach(way, p):
        return NZ // 2 if (way == 0) == (p < 2) else NZ // 2 - 1

    def t_source(way, dist):
        return (z + NZ - dist) % NZ if way == 0 else (z + dist) % NZ

    ONWARD = {0: (2, 1), 2: (4, 3), 4: (6, 5), 6: (7,), 7: (8,)}

    def t_forward(way, dist, p):
        piece = t_piece(t_source(way, dist), p)
        for there in ONWARD.get(dist, ()):
            if there <= reach(way, p):
                to = device(x, y, t_source(way, NZ + dist - there), core)
                send(piece, piece, t_send.at[way], t_recv.at[way, there - 1, p], to)

    for p in range(PIECES):
        for way in (0, 1):
            t_forward(way, 0, p)

    def q_give(a, b):
        to = device((x + a) % NX, (y + b) % NY, z, core)
        send(qblk.at[mine], qblk.at[mine], q_send, q_recv.at[chip], to)

    def q_take(a, b):
        chip_ = ((y + b) % NY) * NX + (x + a) % NX
        s = chip_ * 2 + core
        wait(qblk.at[s], q_recv.at[chip_])
        send(qblk.at[s], qblk.at[s], q_fwd, q_sib, device(x, y, z, sib))

    for a, b in near_chips:
        q_give(a, b)
    corners = [(1, 1), (3, 1), (1, 3)]
    others = [s for s in near_chips if s not in corners] + far_chips
    send(qblk.at[mine], qblk.at[mine], q_fwd, q_sib, device(x, y, z, sib))
    for j in range(1, NY):
        send(qm_ref.at[zl], qmb.at[y], m_send.at[0], m_recv.at[0], device(x, (y + j) % NY, z, core))
    qmb[y] = qm_ref[zl]
    tmb[zl] = tms[y]

    for step, dist in enumerate((2, 1, 4, 3, 6, 5, 7, 8)):
        for p in range(PIECES):
            for way in (0, 1):
                if dist <= reach(way, p):
                    wait(t_piece(t_source(way, dist), p), t_recv.at[way, dist - 1, p])
                    t_forward(way, dist, p)
        if step == 1:
            for a, b in corners:
                q_take(a, b)
            for a, b in far_chips:
                q_give(a, b)
        if 4 <= step < 7:
            for a, b in others[4 * (step - 4):4 * (step - 3)]:
                q_take(a, b)
        if step == NL - 1:
            for j in range(1, NL):
                send(tms.at[y], tmb.at[zl], m_send.at[1], m_recv.at[1], device(x, y, zh * NL + (zl + j) % NL, core))
        if step == NZ // 2 - 2:
            wait(qblk.at[pl.ds(0, CHIPS)], q_sib)
            early = products(1 - zl // 2)

    def dense(v):
        return jnp.concatenate([v[:, c * 128:(c + 1) * 128] for c in range(TB // 128)], axis=0)

    def undense(v):
        return jnp.concatenate([v[c:c + 1, :] for c in range(TB // 128)], axis=1)

    def gather_rows(n, value):
        rsend[n] = value
        rbuf[n, mine] = value

        for peer in plane:
            send(rsend.at[n], rbuf.at[n, mine], r_send.at[n], r_recv.at[n], peer)

    def wait_rows(n):
        wait(rbuf.at[n, pl.ds(0, 2 * CHIPS - 1)], r_recv.at[n])
        return rbuf[n]

    def gather_cols(n, value):
        csend[n] = value
        cbuf[n, z] = value

        for peer in column:
            send(csend.at[n], cbuf.at[n, z], c_send.at[n], c_recv.at[n], peer)

    def wait_cols(n):
        wait(cbuf.at[n, pl.ds(0, NZ - 1)], c_recv.at[n])
        return cbuf[n]

    def lse(parts):
        top = jnp.max(parts, axis=0)
        return top + jnp.log2(jnp.sum(jnp.exp2(parts - top[None]), axis=0))

    def spread_rows(value):
        for k in range(QB // 8):
            cols[k * 8:k * 8 + 8, :] = jnp.broadcast_to(value[:, k:k + 1], (8, 128))

    def wide(r0, rows):
        return jnp.concatenate([cols[pl.ds(r0, rows), :]] * (TB // 128), axis=1)

    (top_a, sum_a), (top_b, sum_b) = early, products(zl // 2)
    tops = jnp.maximum(top_a, top_b)
    sums = sum_a * jnp.exp2(top_a - tops) + sum_b * jnp.exp2(top_b - tops)
    gather_rows(0, tops + jnp.log2(sums))
    send(tblk, tsib, s_send, s_recv, device(x, y, z, sib))

    wait(qmb.at[pl.ds(0, NY - 1)], m_recv.at[0])
    wait(tmb.at[pl.ds(0, NL - 1)], m_recv.at[1])
    mass_q = jnp.zeros((8, 128), F32)
    for b in range(8):
        line = qmb[b // 2, pl.ds(b % 2, 1), :]
        spread = jnp.broadcast_to(line, (128, 128)).T
        for k in range(16):
            mass_q = jnp.where(lane == b * 16 + k, spread[k * 8:k * 8 + 8, :], mass_q)
    mass_t = jnp.concatenate([tmb[i] for i in range(NL)], axis=1)

    first_f = jnp.log2(mass_q) - lse(wait_rows(0))

    spread_rows(first_f)

    def col_max(i, top):
        r0 = pl.multiple_of(i * RB, RB)
        s = plan[pl.ds(r0, RB), :] + wide(r0, RB)
        plan[pl.ds(r0, RB), :] = s
        return jnp.maximum(top, jnp.max(s.reshape(RB // 8, 8, TB), axis=0))

    top8 = lax.fori_loop(0, NB, col_max, jnp.full((8, TB), -jnp.inf, F32), unroll=4)
    top = jnp.max(top8, axis=0, keepdims=True)

    def col_sum(i, acc):
        s = plan[pl.ds(pl.multiple_of(i * RB, RB), RB), :]
        return acc + jnp.sum(jnp.exp2(s - top).reshape(RB // 8, 8, TB), axis=0)

    acc = lax.fori_loop(0, NB, col_sum, jnp.zeros((8, TB), F32), unroll=4)
    gather_cols(0, dense(top + jnp.log2(jnp.sum(acc, axis=0, keepdims=True))))
    first_g = jnp.log2(mass_t) - undense(lse(wait_cols(0)))

    def second_rows(i, sums):
        r0 = pl.multiple_of(i * RB, RB)
        e = jnp.exp2(plan[pl.ds(r0, RB), :] + first_g)
        plan[pl.ds(r0, RB), :] = e
        return pick(sums, i, jnp.sum(e, axis=1, keepdims=True))

    def later_rows(v):
        def body(i, sums):
            e = plan[pl.ds(pl.multiple_of(i * RB, RB), RB), :] * v
            return pick(sums, i, jnp.sum(e, axis=1, keepdims=True))
        return lax.fori_loop(0, NB, body, zero, unroll=4)

    def later_cols():
        def body(i, acc):
            r0 = pl.multiple_of(i * RB, RB)
            e = plan[pl.ds(r0, RB), :] * wide(r0, RB)
            return acc + jnp.sum(e.reshape(RB // 8, 8, TB), axis=0)
        acc = lax.fori_loop(0, NB, body, jnp.zeros((8, TB), F32), unroll=4)
        return dense(jnp.sum(acc, axis=0, keepdims=True))

    gather_rows(1, lax.fori_loop(0, NB, second_rows, zero, unroll=4))
    u = mass_q / jnp.sum(wait_rows(1), axis=0)
    spread_rows(u)
    gather_cols(1, later_cols())
    v = mass_t / undense(jnp.sum(wait_cols(1), axis=0))
    gather_rows(2, later_rows(v))
    u = mass_q / jnp.sum(wait_rows(2), axis=0)
    spread_rows(u)
    gather_cols(2, later_cols())

    f = (first_f + jnp.log2(u)) * POT
    for b in range(8):
        block = jnp.concatenate(
            [jnp.broadcast_to(f[:, b * 16 + k:b * 16 + k + 1], (8, 128)) for k in range(16)], axis=0
        )
        fout[b // 2, pl.ds(b % 2, 1), :] = block.T[0:1, :]
    for j in range(1, NL):
        send(fout.at[y], qpb.at[zl], o_send.at[0], o_recv.at[0], device(x, y, zh * NL + (zl + j) % NL, core))
    qpb[zl] = fout[y]
    v = mass_t / undense(jnp.sum(wait_cols(2), axis=0))

    PB = 2 * QS

    def weights(y_, i, sums):
        c = y_ * NX + i
        r0 = pl.multiple_of(c * PB, PB)
        e = (plan[pl.ds(r0, PB), :] * wide(r0, PB) * v).astype(BF16)
        w[c] = e.reshape(2, QS, TB)
        return pick(sums, c, jnp.sum(e.astype(F32), axis=1, keepdims=True))

    wait(tsib, s_recv)
    sums = zero
    for h in range(NY):
        y_ = (y + (2, 1, 3, 0)[h]) % NY
        sums = lax.fori_loop(0, NX, functools.partial(weights, y_), sums, unroll=2)
        send(w.at[pl.ds(y_ * NX, NX), sib], wsib.at[pl.ds(y_ * NX, NX)], ws_send, ws_recv.at[h], device(x, y, z, sib))

    own, other = tblk[...].reshape(TB, D), tsib[...].reshape(TB, D)
    HD = D // 2
    for h, dy in enumerate((2, 1, 3, 0)):
        y_ = (y + dy) % NY
        a = w[pl.ds(y_ * NX, NX), core].reshape(NX * QS, TB)
        p = jnp.dot(a, own, preferred_element_type=F32)
        wait(wsib.at[pl.ds(y_ * NX, NX)], ws_recv.at[h])
        b = wsib[pl.ds(y_ * NX, NX)].reshape(NX * QS, TB)
        p = p + jnp.dot(b, other, preferred_element_type=F32)
        for f in (0, 1):
            part[f, pl.ds(y_ * NX, NX)] = p[:, f * HD:(f + 1) * HD].reshape(NX, QS, HD)
        for dx in (2, 1, 3, 0):
            x_ = (x + dx) % NX
            if dx:
                send(part.at[0, y_ * NX + x_], got.at[0, y_, x], p_send.at[0], p_recv.at[0, y_], device(x_, y, z, core))
            else:
                got[0, y_, x] = part[0, y_ * NX + x]
            if dy:
                send(part.at[1, y_ * NX + x_], got.at[1, x_, y], p_send.at[1], p_recv.at[1, x_], device(x, y_, z, core))
            else:
                got[1, x_, y] = part[1, y * NX + x_]

    gather_rows(3, sums)

    def second(f, d):
        at = (y + d) % NY if f == 0 else (x + d) % NX
        wait(got.at[f, at, pl.ds(0, 3)], p_recv.at[f, at])
        total_ = jnp.sum(got[f, at], axis=0)
        if d:
            half[f, at] = total_
            to = device(x, at, z, core) if f == 0 else device(at, y, z, core)
            send(half.at[f, at], last.at[f, y if f == 0 else x], h_send.at[f], h_recv.at[f], to)
        else:
            last[f, at] = total_

    for f, d in ((0, 2), (0, 1), (1, 2), (0, 3), (1, 1), (1, 3), (0, 0), (1, 0)):
        second(f, d)

    g = (first_g + jnp.log2(v)) * POT
    for i in range(NL):
        gout[i] = g[:, i * NH * TS:(i + 1) * NH * TS]
    for j in range(1, NY):
        send(gout.at[zl], tpb.at[y], o_send.at[1], o_recv.at[1], device(x, (y + j) % NY, z, core))
    tpb[y] = gout[zl]
    wait(qpb.at[pl.ds(0, NL - 1)], o_recv.at[0])
    wait(tpb.at[pl.ds(0, NY - 1)], o_recv.at[1])
    qp_ref[...] = qpb[...]
    tp_ref[...] = dense(jnp.concatenate([tpb[i] for i in range(NY)], axis=1))

    totals = jnp.sum(wait_rows(3), axis=0)
    spread_rows(totals)
    total = cols[pl.ds(pl.multiple_of(mine * QS, QS), QS), :]
    for f in (0, 1):
        wait(last.at[f, pl.ds(0, 3)], h_recv.at[f])
    full = jnp.concatenate([jnp.sum(last[f], axis=0) for f in (0, 1)], axis=1)
    map_ref[...] = (full / jnp.concatenate([total] * (D // 128), axis=1)).astype(BF16)

    wait(qblk.at[pl.ds(0, CHIPS - 1)], q_send)
    wait(qblk.at[pl.ds(0, CHIPS)], q_fwd)
    for way in (0, 1):
        for p in range(PIECES):
            wait(tblk.at[pl.ds(0, reach(way, p)), pl.ds(p * PIECE, PIECE)], t_send.at[way])
    wait(tblk, s_send)
    wait(wsib, ws_send)
    wait(qmb.at[pl.ds(0, NY - 1)], m_send.at[0])
    wait(tmb.at[pl.ds(0, NL - 1)], m_send.at[1])
    wait(qpb.at[pl.ds(0, NL - 1)], o_send.at[0])
    wait(tpb.at[pl.ds(0, NY - 1)], o_send.at[1])
    for n in range(4):
        wait(rbuf.at[n, pl.ds(0, 2 * CHIPS - 1)], r_send.at[n])
    for n in range(3):
        wait(cbuf.at[n, pl.ds(0, NZ - 1)], c_send.at[n])
    for f in (0, 1):
        wait(part.at[f, pl.ds(0, 3 * NX)], p_send.at[f])
        wait(last.at[f, pl.ds(0, 3)], h_send.at[f])


def local(queries, tools, query_mass, tool_mass):
    vmem = pl.BlockSpec(memory_space=pltpu.VMEM)
    dma, V = pltpu.SemaphoreType.DMA, pltpu.VMEM
    mapped, qp, tp = pl.pallas_call(
        kernel,
        out_shape=(
            jax.ShapeDtypeStruct((QS, D), BF16),
            jax.ShapeDtypeStruct((NL, 2, 128), F32),
            jax.ShapeDtypeStruct((TB // 128, 128), F32),
        ),
        in_specs=[pl.BlockSpec(memory_space=pltpu.HBM)] * 4,
        out_specs=(vmem,) * 3,
        scratch_shapes=[
            V((2 * CHIPS, QS, D), BF16), V((NZ, TS, D), BF16), V((NZ, TS, D), BF16), V((QB, TB), F32),
            V((CHIPS, 2, QS, TB), BF16), V((CHIPS, QS, TB), BF16),
            V((2, CHIPS, QS, D // 2), F32), V((2, 4, 4, QS, D // 2), F32),
            V((2, 4, QS, D // 2), F32), V((2, 4, QS, D // 2), F32),
            V((QB, 128), F32),
            V((NL, 2, 128), F32), V((TB // 128, 128), F32),
            V((4, 8, 128), F32), V((4, 2 * CHIPS, 8, 128), F32), V((3, TB // 128, 128), F32), V((3, NZ, TB // 128, 128), F32),
            V((NY, 2, 128), F32), V((NY, 1, NH * TS), F32), V((NL, 1, NH * TS), F32),
            V((NY, 2, 128), F32), V((NL, 2, 128), F32), V((NL, 1, NH * TS), F32), V((NY, 1, NH * TS), F32),
            dma((4,)), dma, dma((CHIPS,)), dma, dma, dma((2,)), dma((2, NZ // 2, 3)), dma, dma, dma, dma((NY,)),
            dma((2,)), dma((2,)), dma((4,)), dma((4,)), dma((3,)), dma((3,)), dma((2,)), dma((2,)),
            dma((2,)), dma((2, 4)), dma((2,)), dma((2,)),
        ],
        compiler_params=pltpu.CompilerParams(
            collective_id=0, has_side_effects=True, vmem_limit_bytes=60 * 1024 * 1024
        ),
    )(queries, tools, query_mass.reshape(NL, 2, 128), tool_mass.reshape(TB // 128, 128))
    return mapped, qp.reshape(QB), tp.reshape(TB)


def solution(mesh):
    in_specs = (P(("row", "col"), None), P(("col", "row"), None), P("row"), P("col"))
    out_specs = (P(("row", "col"), None), P("row"), P("col"))
    return jax.shard_map(local, mesh=mesh, in_specs=in_specs, out_specs=out_specs, check_vma=False)
```
